32 devices in a mesh: depth: 2 (over x), tile: 16 (over z, y, core).
Axes of the slice: x: 2, y: 2, z: 4, core: 2. Of those that a mesh axis runs over, the one named last changes fastest.
Arguments:
- exit_grad: bfloat16 [64, 256, 2, 256], P('tile', 'depth'), may hold values from -6 to 6
- stored_waves: bfloat16 [4, 64, 256, 2, 256], P('depth', 'tile'), may hold values from -6 to 6
- object_slices: float32 [4, 448, 2, 4096], P('depth', None, None, 'tile'), may hold values from -4 to 4
- propagator_taps: float32 [2, 2, 31], replicated, may hold values from -0.75 to 0.75
- positions: int32 [64, 2], replicated, may hold values from 0 to 255, as said below
- counts: int32 [16], replicated, may hold values from 1 to 4, as said below
Outputs:
- object_grad: bfloat16 [4, 448, 2, 4096], P('depth', None, None, 'tile')
The draws below stay inside these ranges and needn't reach their ends.
Inputs may be any that keep to these rules, and one draw needn't show every extreme that they name: Column 0 is a window's first row, 0 to 192; column 1 is a window's centre column within its tile, 0 to 255. Dead slots hold positions too. `counts`: some tile has exactly 4 live slots and some tile exactly 1.
All inputs are finite; a program needn't handle non-finite values.
Results may differ from the reference program's by a relative error of at most 0.034.
Values may be sent and summed in bfloat16 or wider, within the bound.
No kernel may reach another device: no remote copies, remote signals or barrier semaphores. Data moves between devices by JAX's collectives and lax.ppermute only.
A program may use at most 64 MiB of HBM per device.

```python
import jax
import jax.numpy as jnp
from jax import lax

PROBE = 256
TAPS = 31
CAP = 4
TILE_COLS = 256
ROWS = 448
TILES = 16
SLOTS = 64
SLICES = 4
OBJ_COLS = 4096


def draw_counts(key, part):
    subkeys = jax.random.split(jax.random.fold_in(key, 11), 3)
    draw_level = jax.random.randint(subkeys[0], (TILES,), 0, 100)
    level_cubed = draw_level * draw_level * draw_level
    counts_drawn = 1 + (CAP - 1) * level_cubed // 970299
    busiest = jax.random.randint(subkeys[1], (), 0, TILES)
    lightest = (busiest + 1 + jax.random.randint(subkeys[2], (), 0, TILES - 1)) % TILES
    counts_drawn = counts_drawn.at[busiest].set(CAP)
    counts_drawn = counts_drawn.at[lightest].set(1)
    return counts_drawn.astype(jnp.int32)


def draw_positions(key, part):
    subkeys = jax.random.split(jax.random.fold_in(key, 23), 2)
    row_starts = jax.random.randint(subkeys[0], (SLOTS,), 0, ROWS - PROBE + 1)
    column_starts = jax.random.randint(subkeys[1], (SLOTS,), 0, TILE_COLS)
    last_first = (TILES - 1) * CAP
    row_starts = row_starts.at[0].set(0).at[last_first].set(ROWS - PROBE)
    column_starts = column_starts.at[0].set(0).at[last_first].set(TILE_COLS - 1)
    return jnp.stack([row_starts, column_starts], axis=1).astype(jnp.int32)


def levels(rng, shape, shards, smallest, top_value):
    factor_of = 1.0
    for dim, parts in shards:
        draws = jax.random.uniform(jax.random.fold_in(jax.random.fold_in(rng, 6), dim), (parts,), jnp.float32, smallest / len(shards), top_value / len(shards))
        factor_of = factor_of * jnp.repeat(jnp.exp(draws), shape[dim] // parts).reshape((-1,) + (1,) * (len(shape) - 1 - dim))
    return factor_of


def gaussian(own_key, shape, spread, limit, cuts=(), kind=jnp.bfloat16):
    drawn = jax.random.normal(own_key, shape, jnp.float32) * spread
    if len(cuts) > 0:
        drawn = levels(own_key, shape, cuts, -0.22, 0.18) * drawn
    return jnp.clip(drawn, min=-limit, max=limit).astype(kind)


def setup_inputs(seed: int = 0) -> dict:
    splits = jax.random.split(jax.random.key(seed), 7)
    return {
        "exit_grad": gaussian(splits[0], (SLOTS, PROBE, 2, PROBE), 1.0, 6.0, ((0, 16), (1, 2))),
        "stored_waves": gaussian(splits[1], (SLICES, SLOTS, PROBE, 2, PROBE), 1.0, 6.0, ((0, 2), (1, 16))),
        "object_slices": gaussian(splits[2], (SLICES, ROWS, 2, OBJ_COLS), 0.7, 4.0, ((0, 2), (3, 16)), jnp.float32),
        "propagator_taps": gaussian(splits[3], (2, 2, TAPS), (2 * TAPS) ** -0.5, 0.75, (), jnp.float32),
        "positions": draw_positions(jax.random.fold_in(splits[6], 71), 0),
        "counts": draw_counts(jax.random.fold_in(splits[6], 71), 0),
    }


def band_blocks(propagator_taps, probe_side):
    tap_count = propagator_taps.shape[2]
    centre = tap_count // 2
    places = jnp.arange(probe_side, dtype=jnp.int32)
    offset = places[None, :] - places[:, None] + centre
    onehot = (offset.reshape(1, probe_side * probe_side) == jnp.arange(tap_count, dtype=jnp.int32)[:, None]).astype(jnp.float32)
    flat_taps = jnp.dot(propagator_taps.reshape(4, tap_count), onehot, precision=lax.Precision.HIGHEST, preferred_element_type=jnp.float32)
    matrices = flat_taps.reshape(2, 2, probe_side, probe_side)
    y_real, y_imag = matrices[0, 0], matrices[0, 1]
    x_real, x_imag = matrices[1, 0], matrices[1, 1]
    column_block = jnp.concatenate([jnp.concatenate([x_real, -x_imag], 1), jnp.concatenate([x_imag, x_real], 1)], 0).astype(jnp.bfloat16)
    row_block = jnp.concatenate([y_real.T, y_imag.T], 0).astype(jnp.bfloat16)
    return column_block, row_block


def propagate(wave_block, column_block, row_block):
    probe_side = wave_block.shape[1]
    flat_waves = wave_block.reshape(wave_block.shape[0], probe_side, 2 * probe_side).astype(jnp.float32)
    mixed = jnp.einsum("mrc,cd->mrd", flat_waves, column_block.astype(jnp.float32), precision=lax.Precision.HIGHEST).astype(jnp.bfloat16)
    stacked = jnp.einsum("ar,mrd->mad", row_block.astype(jnp.float32), mixed.astype(jnp.float32), precision=lax.Precision.HIGHEST)
    upper_half = stacked[:, :probe_side]
    lower_half = stacked[:, probe_side:]
    wave_real = upper_half[:, :, :probe_side] + lower_half[:, :, probe_side:]
    wave_imag = upper_half[:, :, probe_side:] - lower_half[:, :, :probe_side]
    return wave_real, wave_imag


def reference(exit_grad, stored_waves, object_slices, propagator_taps, positions, counts):
    probe_side = exit_grad.shape[1]
    half_side = probe_side // 2
    column_block, row_block = band_blocks(propagator_taps, probe_side)
    slot_ids = jnp.arange(positions.shape[0], dtype=jnp.int32)
    slot_owner = slot_ids // CAP
    live_weight = (slot_ids % CAP < counts[slot_owner]).astype(jnp.float32)
    row_starts = positions[:, 0].astype(jnp.int32)
    column_starts = (slot_owner * TILE_COLS + positions[:, 1]).astype(jnp.int32)
    row_count = object_slices.shape[1]
    wave_now = exit_grad
    slice_grads = []
    for slice_index in range(SLICES - 1, -1, -1):
        slab = object_slices[slice_index]
        extended = jnp.concatenate([slab[:, :, OBJ_COLS - half_side:], slab, slab[:, :, :half_side]], axis=2)

        def per_slot(accumulator, slot_item):
            wave_one, stored, row_start, col_start, weight = slot_item
            wave_real, wave_imag = propagate(wave_one[None], column_block, row_block)
            wave_real = wave_real[0]
            wave_imag = wave_imag[0]
            zero_index = jnp.zeros((), jnp.int32)
            window = lax.dynamic_slice(extended, (row_start, zero_index, col_start), (probe_side, 2, probe_side))
            stored_real = stored[:, 0].astype(jnp.float32)
            stored_imag = stored[:, 1].astype(jnp.float32)
            grad_real = stored_real * wave_real + stored_imag * wave_imag
            grad_imag = stored_real * wave_imag - stored_imag * wave_real
            term = jnp.stack([grad_real, grad_imag], 1) * weight
            region = lax.dynamic_slice(accumulator, (row_start, zero_index, col_start), (probe_side, 2, probe_side))
            accumulator = lax.dynamic_update_slice(accumulator, region + term, (row_start, zero_index, col_start))
            obj_real = window[:, 0]
            obj_imag = window[:, 1]
            out_wave = jnp.stack([obj_real * wave_real + obj_imag * wave_imag, obj_real * wave_imag - obj_imag * wave_real], 1).astype(jnp.bfloat16)
            return accumulator, out_wave

        start_acc = jnp.zeros((row_count, 2, OBJ_COLS + probe_side), jnp.float32)
        accumulator, wave_now = lax.scan(per_slot, start_acc, (wave_now, stored_waves[slice_index], row_starts, column_starts, live_weight))
        owned_part = accumulator[:, :, half_side:half_side + OBJ_COLS]
        owned_part = owned_part.at[:, :, :half_side].add(accumulator[:, :, OBJ_COLS + half_side:])
        owned_part = owned_part.at[:, :, OBJ_COLS - half_side:].add(accumulator[:, :, :half_side])
        slice_grads.append(owned_part.astype(jnp.bfloat16))
    return jnp.stack(slice_grads[::-1])
```

```python
import functools

import jax
import jax.numpy as jnp
from jax import lax
from jax.experimental import pallas as pl
from jax.experimental.pallas import tpu as pltpu
from jax.sharding import PartitionSpec as P

LANES = 128
CHUNK = 64
F32 = jnp.float32
BF16 = jnp.bfloat16
VMEM = pl.BlockSpec(memory_space=pltpu.VMEM)
SMEM = pl.BlockSpec(memory_space=pltpu.SMEM)


def params(mib):
    return pltpu.CompilerParams(vmem_limit_bytes=mib << 20)


def as_rows(x):
    *lead, parts, columns = x.shape
    tiles = columns // LANES
    split = x.reshape(*lead, parts, tiles, LANES)
    return jnp.swapaxes(split, -3, -2).reshape(-1, LANES)


def from_rows(x, shape):
    *lead, parts, columns = shape
    tiles = columns // LANES
    split = x.reshape(*lead, tiles, parts, LANES)
    return jnp.swapaxes(split, -3, -2).reshape(shape)


def row_ids(start, rows):
    return lax.broadcasted_iota(jnp.int32, (rows, LANES), 0) + start


def lane_ids(rows):
    return lax.broadcasted_iota(jnp.int32, (rows, LANES), 1)


class Place:
    def __init__(self, meta, j, cap):
        tile = meta[1]
        self.row = meta[4 + (tile * cap + j) * 2]
        self.col = meta[5 + (tile * cap + j) * 2]

    def rows_first(self, start, rows):
        return row_ids(start, rows) >= self.row

    def cols_first(self, column_tile, rows):
        return lane_ids(rows) + column_tile * LANES >= self.col


def edges_kernel(obj, left_edge, right_edge):
    slices, parts, rows, _ = left_edge.shape
    for s in range(slices):
        for c in range(parts):
            base = s * rows * 4
            left_edge[s, c] = obj[pl.ds(base + c, rows, stride=4), :].astype(BF16)
            right_edge[s, c] = obj[pl.ds(base + 2 + c, rows, stride=4), :].astype(BF16)


def setup_kernel(cap, taps_of, meta, taps, stored, planes, col_mat, row_mat, blocks, wide):
    j = pl.program_id(0)
    s = pl.program_id(1)
    side = planes.shape[3]
    tap_count, centre = taps_of

    @pl.when((j == 0) & (s == 0))
    def _():
        def build(i, carry):
            first = pl.multiple_of(i * 32, 32)
            diff = lax.broadcasted_iota(jnp.int32, (32, LANES), 1) - row_ids(first, 32)
            for b, shift in enumerate((0, LANES, -LANES)):
                total = [jnp.zeros((32, LANES), F32) for _ in range(4)]
                for k in range(tap_count):
                    hit = diff + shift == k - centre
                    for m in range(4):
                        index = k if m < 2 else tap_count - 1 - k
                        total[m] = jnp.where(hit, taps[(m ^ 2) * tap_count + index], total[m])
                for m in range(4):
                    blocks[m, b, pl.ds(first, 32), :] = total[m]
            return carry

        lax.fori_loop(0, LANES // 32, build, 0)

    live = j < meta[2]
    place = Place(meta, j, cap)

    @pl.when(live & (s == 0))
    def _():
        def fill(i, carry):
            first = pl.multiple_of(i * 32, 32)
            for at, m0 in ((place.col, 0), (place.row, 2)):
                for tr in range(2):
                    for tc in range(2):
                        row_side = row_ids(first, 32) + tr * LANES >= at
                        col_side = lane_ids(32) + tc * LANES >= at
                        same = row_side == col_side
                        values = []
                        for m in (m0, m0 + 1):
                            if tr == tc:
                                near, far = blocks[m, 0, pl.ds(first, 32), :], 0.0
                            else:
                                near = blocks[m, 1 + tr, pl.ds(first, 32), :]
                                far = blocks[m, 2 - tr, pl.ds(first, 32), :]
                            values.append(jnp.where(same, near, far))
                        re, im = values
                        rows = pl.ds(pl.multiple_of(first + tr * LANES, 32), 32)
                        low = pl.ds(pl.multiple_of(first + tr * LANES + side, 32), 32)
                        near_cols = pl.ds(tc * LANES, LANES)
                        far_cols = pl.ds(tc * LANES + side, LANES)
                        if m0 == 0:
                            col_mat[0, rows, near_cols] = re.astype(BF16)
                            col_mat[0, rows, far_cols] = (-im).astype(BF16)
                            col_mat[0, low, near_cols] = im.astype(BF16)
                            col_mat[0, low, far_cols] = re.astype(BF16)
                        else:
                            row_mat[0, rows, near_cols] = re.astype(BF16)
                            row_mat[0, rows, far_cols] = im.astype(BF16)
            return carry

        lax.fori_loop(0, LANES // 32, fill, 0)

    @pl.when(live)
    def _():
        put_in_place(place, [(stored, 0, side)], wide, lambda c, rows, v: planes.__setitem__((0, 0, c, rows), v))


def put_in_place(place, sources, wide, write):
    first_row = 0
    for ref, start, count in sources:
        wide[pl.ds(place.row * 4 + first_row * 4, count * 4), :] = ref[pl.ds(start, count * 4), :].astype(F32)
        first_row += count
    side = first_row

    def move(i, carry):
        a = pl.multiple_of(i * CHUNK, CHUNK)
        keep = place.rows_first(a, CHUNK)
        for c in range(2):
            halves = []
            for ct in range(2):
                upper = wide[pl.ds(a * 4 + ct * 2 + c, CHUNK, stride=4), :]
                lower = wide[pl.ds((a + side) * 4 + ct * 2 + c, CHUNK, stride=4), :]
                halves.append(jnp.where(keep, upper, lower))
            both = jnp.concatenate(halves, axis=1)
            write(c, pl.ds(a, CHUNK), pltpu.roll(both, place.col, 1).astype(BF16))
        return carry

    lax.fori_loop(0, side // CHUNK, move, 0)


def back(wave, col_mat, row_mat, rhs, h_buf):
    side = wave.shape[0]
    mixed = jnp.dot(wave[...], col_mat[0], preferred_element_type=F32).astype(BF16)
    rhs[:side, :] = mixed
    rhs[side:, :side] = mixed[:, side:]
    rhs[side:, side:] = -mixed[:, :side]
    h_buf[...] = jnp.dot(row_mat[0], rhs[...], preferred_element_type=F32)


def window_part(place, obj, from_left, from_right, s, c, ct, a, rows, side):
    total_rows = from_left.shape[2]
    own_tile = 1 - ct
    halo = from_left if ct == 0 else from_right

    def at(first):
        own = obj[pl.ds((s * total_rows + first) * 4 + own_tile * 2 + c, rows, stride=4), :]
        other = halo[s, c, pl.ds(first, rows), :].astype(F32)
        first_cols = place.cols_first(ct, rows)
        return jnp.where(first_cols, other, own) if ct == 0 else jnp.where(first_cols, own, other)

    second = pl.multiple_of(jnp.minimum(a + side, total_rows - rows), rows)
    return jnp.where(place.rows_first(a, rows), at(a), at(second))


def chain_slices(place, s_first, slices, refs, on_chunk, need_last_wave):
    obj, from_left, from_right, col_mat, row_mat, wave, rhs, h_buf = refs
    side = wave.shape[0]

    def one_slice(i, carry):
        s = slices - 1 - i
        back(wave, col_mat, row_mat, rhs, h_buf)

        def chunk(k, inner):
            a = pl.multiple_of(k * CHUNK, CHUNK)
            rows = pl.ds(a, CHUNK)
            for ct in range(2):
                near = pl.ds(ct * LANES, LANES)
                far = pl.ds(ct * LANES + side, LANES)
                h_re = h_buf[rows, near]
                h_im = h_buf[rows, far]
                o_re = window_part(place, obj, from_left, from_right, s, 0, ct, a, CHUNK, side)
                o_im = window_part(place, obj, from_left, from_right, s, 1, ct, a, CHUNK, side)
                wave[rows, near] = (o_re * h_re + o_im * h_im).astype(BF16)
                wave[rows, far] = (o_re * h_im - o_im * h_re).astype(BF16)
                if on_chunk is not None:
                    on_chunk(s, ct, a, h_re, h_im)
            return inner

        lax.fori_loop(0, side // CHUNK, chunk, 0)
        return carry

    lax.fori_loop(0, slices, one_slice, 0)


def load_exit(place, j, exits, wide, wave):
    side = wave.shape[0]
    count = side // len(exits)
    sources = [(ref, j * count * 4, count) for ref in exits]

    def write(c, rows, value):
        wave[rows, pl.ds(c * side, side)] = value

    put_in_place(place, sources, wide, write)


def forward_kernel(cap, j, group, last, n_in, *refs):
    meta, obj, from_left, from_right, col_mat, row_mat = refs[:6]
    incoming = refs[6 : 6 + n_in]
    out, wide, rhs, h_buf = refs[6 + n_in :]
    slices = from_left.shape[0]

    @pl.when(meta[0] == group)
    def _():
        place = Place(meta, j, cap)
        if last:
            load_exit(place, j, incoming, wide, out)
        else:
            out[...] = incoming[0][...]
        chain_slices(place, 0, slices, (obj, from_left, from_right, col_mat, row_mat, out, rhs, h_buf), None, True)


def grad_kernel(cap, groups, j, first, final, n_exits, *refs):
    meta, obj, from_left, from_right, col_mat, row_mat, planes, received = refs[:8]
    exits = refs[8 : 8 + n_exits]
    rest = refs[8 + n_exits :]
    old, rest = (None, rest) if first else (rest[0], rest[1:])
    sums, wide, wave, rhs, h_buf = rest
    slices = from_left.shape[0]
    total_rows = from_left.shape[2]
    side = wave.shape[0]
    place = Place(meta, j, cap)
    sums[...] = jnp.zeros(sums.shape, F32) if first else old[...]

    @pl.when(meta[0] == groups - 1)
    def _():
        load_exit(place, j, exits, wide, wave)

    @pl.when(meta[0] != groups - 1)
    def _():
        wave[...] = received[...]

    def on_chunk(s, ct, a, h_re, h_im):
        rows = pl.ds(a, CHUNK)
        cols = pl.ds(ct * LANES, LANES)
        st_re = planes[0, s, 0, rows, cols].astype(F32)
        st_im = planes[0, s, 1, rows, cols].astype(F32)
        g = (st_re * h_re + st_im * h_im, st_re * h_im - st_im * h_re)
        up = place.rows_first(a, CHUNK)
        left = place.cols_first(ct, CHUNK)
        for c in range(2):
            for tile, cols_in in ((ct, left), (ct + 2, ~left)):
                sums[s, c, tile, rows, :] += jnp.where(up & cols_in, g[c], 0.0)

        @pl.when(a + side < total_rows)
        def _():
            lower = pl.ds(pl.multiple_of(a + side, CHUNK), CHUNK)
            for c in range(2):
                for tile, cols_in in ((ct, left), (ct + 2, ~left)):
                    sums[s, c, tile, lower, :] += jnp.where(~up & cols_in, g[c], 0.0)

    chain_slices(place, 0, slices, (obj, from_left, from_right, col_mat, row_mat, wave, rhs, h_buf), on_chunk, False)


def rims_kernel(left_sums, right_sums, left_rim, right_rim):
    left_rim[...] = left_sums[:, :, 0].astype(BF16)
    right_rim[...] = right_sums[:, :, 0].astype(BF16)


def close_kernel(sums, from_left, from_right, out, mix):
    slices, parts, _, rows, _ = sums.shape
    for s in range(slices):
        for c in range(parts):
            for ct, other in ((0, from_left), (1, from_right)):
                total = sums[s, c, 1 + ct] + other[s, c].astype(F32)
                mix[pl.ds(s * rows * 4 + ct * 2 + c, rows, stride=4), :] = total
    out[...] = mix[...].astype(BF16)


def on_device(exit_grad, stored_waves, object_slices, propagator_taps, positions, counts):
    slices, cap, side = stored_waves.shape[:3]
    rows = object_slices.shape[1]
    groups = lax.axis_size("depth")
    tiles = lax.axis_size("tile")
    tap_count = propagator_taps.shape[2]
    group_index = lax.axis_index("depth")
    tile_index = lax.axis_index("tile")
    my_count = lax.dynamic_index_in_dim(counts, tile_index, 0, False)
    head = jnp.stack([group_index, tile_index, my_count, my_count]).astype(jnp.int32)
    meta = jnp.concatenate([head, positions.astype(jnp.int32).reshape(-1)])
    up = [(i, (i + 1) % tiles) for i in range(tiles)]
    down = [(i, (i - 1) % tiles) for i in range(tiles)]

    received_exits = [lax.ppermute(exit_grad, "depth", [(g, groups - 1)]) for g in range(groups - 1)]
    exits = [as_rows(e) for e in received_exits + [exit_grad]]
    obj = as_rows(object_slices)

    edge_shape = jax.ShapeDtypeStruct((slices, 2, rows, LANES), BF16)
    left_edge, right_edge = pl.pallas_call(
        edges_kernel,
        out_shape=(edge_shape, edge_shape),
        in_specs=[VMEM],
        out_specs=(VMEM, VMEM),
        compiler_params=params(16),
        name="edges",
    )(obj)
    from_left = lax.ppermute(right_edge, "tile", up)
    from_right = lax.ppermute(left_edge, "tile", down)

    planes, col_mats, row_mats = pl.pallas_call(
        functools.partial(setup_kernel, cap, (tap_count, tap_count // 2)),
        out_shape=(
            jax.ShapeDtypeStruct((cap, slices, 2, side, side), BF16),
            jax.ShapeDtypeStruct((cap, 2 * side, 2 * side), BF16),
            jax.ShapeDtypeStruct((cap, side, 2 * side), BF16),
        ),
        grid=(cap, slices),
        in_specs=[
            SMEM,
            SMEM,
            pl.BlockSpec((side * 4, LANES), lambda j, s: (s * cap + j, 0)),
        ],
        out_specs=(
            pl.BlockSpec((1, 1, 2, side, side), lambda j, s: (j, s, 0, 0, 0)),
            pl.BlockSpec((1, 2 * side, 2 * side), lambda j, s: (j, 0, 0)),
            pl.BlockSpec((1, side, 2 * side), lambda j, s: (j, 0, 0)),
        ),
        scratch_shapes=[
            pltpu.VMEM((4, 3, LANES, LANES), F32),
            pltpu.VMEM((2 * side * 4, LANES), F32),
        ],
        compiler_params=params(16),
        name="setup",
    )(meta, propagator_taps.reshape(-1), as_rows(stored_waves))

    def at_slot(j, *block):
        return pl.BlockSpec((1, *block), lambda i: (j,) + (0,) * len(block))

    wide_scratch = pltpu.VMEM((2 * side * 4, LANES), F32)
    rhs_scratch = pltpu.VMEM((2 * side, 2 * side), BF16)
    h_scratch = pltpu.VMEM((side, 2 * side), F32)
    wave_shape = jax.ShapeDtypeStruct((side, 2 * side), BF16)
    sums_shape = jax.ShapeDtypeStruct((slices, 2, 4, rows, LANES), F32)

    def forward(j, group, incoming):
        last = group == groups - 1
        return pl.pallas_call(
            functools.partial(forward_kernel, cap, j, group, last, len(incoming)),
            out_shape=wave_shape,
            grid=(1,),
            in_specs=[SMEM, VMEM, VMEM, VMEM, at_slot(j, 2 * side, 2 * side), at_slot(j, side, 2 * side)]
            + [VMEM] * len(incoming),
            out_specs=VMEM,
            scratch_shapes=[wide_scratch, rhs_scratch, h_scratch],
            compiler_params=params(24),
            name=f"forward{j}",
        )(meta, obj, from_left, from_right, col_mats, row_mats, *incoming)

    def gradient(j, received, sums):
        old = [] if sums is None else [sums]
        return pl.pallas_call(
            functools.partial(grad_kernel, cap, groups, j, sums is None, False, len(exits)),
            out_shape=sums_shape,
            grid=(1,),
            in_specs=[SMEM, VMEM, VMEM, VMEM, at_slot(j, 2 * side, 2 * side), at_slot(j, side, 2 * side)]
            + [at_slot(j, slices, 2, side, side), VMEM]
            + [VMEM] * (len(exits) + len(old)),
            out_specs=VMEM,
            scratch_shapes=[wide_scratch, pltpu.VMEM((side, 2 * side), BF16), rhs_scratch, h_scratch],
            input_output_aliases={} if sums is None else {8 + len(exits): 0},
            compiler_params=params(32),
            name=f"gradient{j}",
        )(meta, obj, from_left, from_right, col_mats, row_mats, planes, received, *exits, *old)

    def with_live(live):
        def run():
            waves = [exits] * live
            received = [None] * live
            for group in range(groups - 1, 0, -1):
                for j in range(live):
                    incoming = waves[j] if group == groups - 1 else [waves[j]]
                    sent = forward(j, group, incoming)
                    arrived = lax.ppermute(sent, "depth", [(group, group - 1)])
                    waves[j] = arrived
                    mine = group_index == group - 1
                    received[j] = arrived if received[j] is None else jnp.where(mine, arrived, received[j])
            sums = None
            for j in range(live):
                wave = jnp.zeros((side, 2 * side), BF16) if received[j] is None else received[j]
                sums = gradient(j, wave, sums)
            return sums

        return run

    sums = lax.switch(my_count - 1, [with_live(n + 1) for n in range(cap)])

    def tile_of(index):
        return pl.BlockSpec((slices, 2, 1, rows, LANES), lambda i: (0, 0, index, 0, 0))

    left_rim, right_rim = pl.pallas_call(
        rims_kernel,
        out_shape=(edge_shape, edge_shape),
        grid=(1,),
        in_specs=[tile_of(0), tile_of(3)],
        out_specs=(VMEM, VMEM),
        compiler_params=params(16),
        name="rims",
    )(sums, sums)
    sums_left = lax.ppermute(right_rim, "tile", up)
    sums_right = lax.ppermute(left_rim, "tile", down)
    out_rows = pl.pallas_call(
        close_kernel,
        out_shape=jax.ShapeDtypeStruct((slices * rows * 4, LANES), BF16),
        in_specs=[VMEM, VMEM, VMEM],
        out_specs=VMEM,
        scratch_shapes=[pltpu.VMEM((slices * rows * 4, LANES), F32)],
        compiler_params=params(32),
        name="close",
    )(sums, sums_left, sums_right)
    return from_rows(out_rows, (slices, rows, 2, 2 * LANES))


def solution(mesh):
    return jax.shard_map(
        on_device,
        mesh=mesh,
        in_specs=(
            P("tile", "depth", None, None),
            P("depth", "tile", None, None, None),
            P("depth", None, None, "tile"),
            P(),
            P(),
            P(),
        ),
        out_specs=P("depth", None, None, "tile"),
        check_vma=False,
    )
```

```python
import functools

import jax
import jax.numpy as jnp
from jax import lax
from jax.experimental import pallas as pl
from jax.experimental.pallas import tpu as pltpu
from jax.sharding import PartitionSpec as P

LANES = 128
CHUNK = 64
F32 = jnp.float32
BF16 = jnp.bfloat16
VMEM = pl.BlockSpec(memory_space=pltpu.VMEM)
SMEM = pl.BlockSpec(memory_space=pltpu.SMEM)


def params(mib):
    return pltpu.CompilerParams(vmem_limit_bytes=mib << 20)


def as_rows(x):
    *lead, parts, columns = x.shape
    tiles = columns // LANES
    split = x.reshape(*lead, parts, tiles, LANES)
    return jnp.swapaxes(split, -3, -2).reshape(-1, LANES)


def from_rows(x, shape):
    *lead, parts, columns = shape
    tiles = columns // LANES
    split = x.reshape(*lead, tiles, parts, LANES)
    return jnp.swapaxes(split, -3, -2).reshape(shape)


def row_ids(start, rows):
    return lax.broadcasted_iota(jnp.int32, (rows, LANES), 0) + start


def lane_ids(rows):
    return lax.broadcasted_iota(jnp.int32, (rows, LANES), 1)


class Place:
    def __init__(self, at, positions, j, cap):
        self.row = positions[0, at[1] * cap + j]
        self.col = positions[1, at[1] * cap + j]

    def rows_first(self, start, rows):
        return row_ids(start, rows) >= self.row

    def cols_first(self, column_tile, rows):
        return lane_ids(rows) + column_tile * LANES >= self.col


def edges_kernel(at, counts, obj, left_edge, right_edge, my_count):
    my_count[0] = counts[at[1]]
    slices, parts, rows, _ = left_edge.shape
    for s in range(slices):
        for c in range(parts):
            base = s * rows * 4
            left_edge[s, c] = obj[pl.ds(base + c, rows, stride=4), :].astype(BF16)
            right_edge[s, c] = obj[pl.ds(base + 2 + c, rows, stride=4), :].astype(BF16)


def build_blocks(taps, blocks):
    tap_count = taps.shape[2]
    centre = tap_count // 2
    step = 32

    def tap(m, k):
        return taps[1, m, k] if m < 2 else taps[0, m - 2, tap_count - 1 - k]

    def build(block, first, shift, ks):
        diff = lane_ids(step) - row_ids(first, step) + shift
        total = [jnp.zeros((step, LANES), F32) for _ in range(4)]
        for k in ks:
            hit = diff == k - centre
            for m in range(4):
                total[m] = jnp.where(hit, tap(m, k), total[m])
        for m in range(4):
            blocks[m, block, pl.ds(first, step), :] = total[m]

    def diagonal(i, carry):
        build(0, pl.multiple_of(i * step, step), 0, range(tap_count))
        return carry

    lax.fori_loop(0, LANES // step, diagonal, 0)
    for first in range(0, LANES, step):
        build(1, first, LANES, range(centre + 1, tap_count) if first + step == LANES else ())
        build(2, first, -LANES, range(centre) if first == 0 else ())


def place_matrices(place, j, blocks, col_mat, row_mat):
    side = row_mat.shape[1]
    step = 32

    def fill(i, carry):
        first = pl.multiple_of(i * step, step)
        for seam, m0 in ((place.col, 0), (place.row, 2)):
            for tr in range(2):
                for tc in range(2):
                    row_side = row_ids(first, step) + tr * LANES >= seam
                    col_side = lane_ids(step) + tc * LANES >= seam
                    same = row_side == col_side
                    values = []
                    for m in (m0, m0 + 1):
                        if tr == tc:
                            near, far = blocks[m, 0, pl.ds(first, step), :], 0.0
                        else:
                            near = blocks[m, 1 + tr, pl.ds(first, step), :]
                            far = blocks[m, 2 - tr, pl.ds(first, step), :]
                        values.append(jnp.where(same, near, far))
                    re, im = values
                    rows = pl.ds(pl.multiple_of(first + tr * LANES, step), step)
                    low = pl.ds(pl.multiple_of(first + tr * LANES + side, step), step)
                    near_cols = pl.ds(tc * LANES, LANES)
                    far_cols = pl.ds(tc * LANES + side, LANES)
                    if m0 == 0:
                        col_mat[j, rows, near_cols] = re.astype(BF16)
                        col_mat[j, rows, far_cols] = (-im).astype(BF16)
                        col_mat[j, low, near_cols] = im.astype(BF16)
                        col_mat[j, low, far_cols] = re.astype(BF16)
                    else:
                        row_mat[j, rows, near_cols] = re.astype(BF16)
                        row_mat[j, rows, far_cols] = im.astype(BF16)
        return carry

    lax.fori_loop(0, LANES // step, fill, 0)


def setup_kernel(at, positions, counts, taps, stored, planes, col_mat, row_mat, blocks, wide):
    cap, slices, _, side, _ = planes.shape
    build_blocks(taps, blocks)

    def slot(j, carry):
        place = Place(at, positions, j, cap)
        place_matrices(place, j, blocks, col_mat, row_mat)

        def one_slice(s, inner):
            def write(c, rows, value):
                planes[j, s, c, rows] = value

            start = pl.multiple_of((s * cap + j) * side * 4, side * 4)
            put_in_place(place, [(stored, start, side)], wide, write)
            return inner

        return lax.fori_loop(0, slices, one_slice, carry)

    lax.fori_loop(0, counts[at[1]], slot, 0)


def put_in_place(place, sources, wide, write):
    first_row = 0
    for ref, start, count in sources:
        wide[pl.ds(place.row * 4 + first_row * 4, count * 4), :] = ref[pl.ds(start, count * 4), :].astype(F32)
        first_row += count
    side = first_row

    def move(i, carry):
        a = pl.multiple_of(i * CHUNK, CHUNK)
        keep = place.rows_first(a, CHUNK)
        for c in range(2):
            halves = []
            for ct in range(2):
                upper = wide[pl.ds(a * 4 + ct * 2 + c, CHUNK, stride=4), :]
                lower = wide[pl.ds((a + side) * 4 + ct * 2 + c, CHUNK, stride=4), :]
                halves.append(jnp.where(keep, upper, lower))
            both = jnp.concatenate(halves, axis=1)
            write(c, pl.ds(a, CHUNK), pltpu.roll(both, place.col, 1).astype(BF16))
        return carry

    lax.fori_loop(0, side // CHUNK, move, 0)


def back(j, wave, col_mat, row_mat, rhs, h_buf):
    side = wave.shape[0]
    mixed = jnp.dot(wave[...], col_mat[j], preferred_element_type=F32).astype(BF16)
    rhs[:side, :] = mixed
    rhs[side:, :side] = mixed[:, side:]
    rhs[side:, side:] = -mixed[:, :side]
    h_buf[...] = jnp.dot(row_mat[j], rhs[...], preferred_element_type=F32)


def window_part(place, obj, from_left, from_right, s, c, ct, a, rows, side):
    total_rows = from_left.shape[2]
    own_tile = 1 - ct
    halo = from_left if ct == 0 else from_right

    def at(first):
        own = obj[pl.ds((s * total_rows + first) * 4 + own_tile * 2 + c, rows, stride=4), :]
        other = halo[s, c, pl.ds(first, rows), :].astype(F32)
        first_cols = place.cols_first(ct, rows)
        return jnp.where(first_cols, other, own) if ct == 0 else jnp.where(first_cols, own, other)

    second = pl.multiple_of(jnp.minimum(a + side, total_rows - rows), rows)
    return jnp.where(place.rows_first(a, rows), at(a), at(second))


def chain_slices(place, j, slices, refs, on_chunk):
    obj, from_left, from_right, col_mat, row_mat, wave, rhs, h_buf = refs
    side = wave.shape[0]

    def one_slice(i, carry):
        s = slices - 1 - i
        back(j, wave, col_mat, row_mat, rhs, h_buf)

        def chunk(k, inner):
            a = pl.multiple_of(k * CHUNK, CHUNK)
            rows = pl.ds(a, CHUNK)
            for ct in range(2):
                near = pl.ds(ct * LANES, LANES)
                far = pl.ds(ct * LANES + side, LANES)
                h_re = h_buf[rows, near]
                h_im = h_buf[rows, far]
                o_re = window_part(place, obj, from_left, from_right, s, 0, ct, a, CHUNK, side)
                o_im = window_part(place, obj, from_left, from_right, s, 1, ct, a, CHUNK, side)
                wave[rows, near] = (o_re * h_re + o_im * h_im).astype(BF16)
                wave[rows, far] = (o_re * h_im - o_im * h_re).astype(BF16)
                if on_chunk is not None:
                    on_chunk(s, ct, a, h_re, h_im)
            return inner

        lax.fori_loop(0, side // CHUNK, chunk, 0)
        return carry

    lax.fori_loop(0, slices, one_slice, 0)


def load_exit(place, j, exits, wide, wave):
    side = wave.shape[0]
    count = side // len(exits)
    sources = [(ref, j * count * 4, count) for ref in exits]

    def write(c, rows, value):
        wave[rows, pl.ds(c * side, side)] = value

    put_in_place(place, sources, wide, write)


def forward_kernel(j, group, last, n_in, *refs):
    at, positions, obj, from_left, from_right, col_mat, row_mat = refs[:7]
    incoming = refs[7 : 7 + n_in]
    out, wide, rhs, h_buf = refs[7 + n_in :]
    slices = from_left.shape[0]

    @pl.when(at[0] == group)
    def _():
        place = Place(at, positions, j, col_mat.shape[0])
        if last:
            load_exit(place, j, incoming, wide, out)
        else:
            out[...] = incoming[0][...]
        chain_slices(place, j, slices, (obj, from_left, from_right, col_mat, row_mat, out, rhs, h_buf), None)


def grad_kernel(groups, j, first, n_exits, *refs):
    at, positions, obj, from_left, from_right, col_mat, row_mat, planes, received = refs[:9]
    exits = refs[9 : 9 + n_exits]
    rest = refs[9 + n_exits :]
    sums, wide, wave, rhs, h_buf = rest if first else rest[1:]
    slices = from_left.shape[0]
    total_rows = from_left.shape[2]
    side = wave.shape[0]
    place = Place(at, positions, j, col_mat.shape[0])
    if first:
        sums[...] = jnp.zeros(sums.shape, F32)

    @pl.when(at[0] == groups - 1)
    def _():
        load_exit(place, j, exits, wide, wave)

    @pl.when(at[0] != groups - 1)
    def _():
        wave[...] = received[...]

    def on_chunk(s, ct, a, h_re, h_im):
        rows = pl.ds(a, CHUNK)
        cols = pl.ds(ct * LANES, LANES)
        st_re = planes[j, s, 0, rows, cols].astype(F32)
        st_im = planes[j, s, 1, rows, cols].astype(F32)
        g = (st_re * h_re + st_im * h_im, st_re * h_im - st_im * h_re)
        up = place.rows_first(a, CHUNK)
        left = place.cols_first(ct, CHUNK)
        for c in range(2):
            for tile, cols_in in ((ct, left), (ct + 2, ~left)):
                sums[s, c, tile, rows, :] += jnp.where(up & cols_in, g[c], 0.0)

        @pl.when(a + side < total_rows)
        def _():
            lower = pl.ds(pl.multiple_of(a + side, CHUNK), CHUNK)
            for c in range(2):
                for tile, cols_in in ((ct, left), (ct + 2, ~left)):
                    sums[s, c, tile, lower, :] += jnp.where(~up & cols_in, g[c], 0.0)

    chain_slices(place, j, slices, (obj, from_left, from_right, col_mat, row_mat, wave, rhs, h_buf), on_chunk)


def rims_kernel(sums, left_rim, right_rim, own):
    left_rim[...] = sums[:, :, 0].astype(BF16)
    right_rim[...] = sums[:, :, 3].astype(BF16)
    own[...] = sums[:, :, 1:3].astype(BF16)


def close_kernel(own, from_left, from_right, out, mix):
    slices, parts, _, rows, _ = own.shape
    for s in range(slices):
        for c in range(parts):
            for ct, other in ((0, from_left), (1, from_right)):
                total = own[s, c, ct].astype(F32) + other[s, c].astype(F32)
                mix[pl.ds(s * rows * 4 + ct * 2 + c, rows, stride=4), :] = total
    out[...] = mix[...].astype(BF16)


def near(x):
    return pltpu.with_memory_space_constraint(x, pltpu.VMEM)


def kernel_call(body, scalars, arrays, out, scratch=(), aliases=None, mib=8, name=None):
    single = not isinstance(out, tuple)
    outs = (out,) if single else out
    specs = tuple(SMEM if o.memory_space == pltpu.SMEM else VMEM for o in outs)
    return pl.pallas_call(
        body,
        out_shape=out,
        in_specs=[SMEM] * len(scalars) + [VMEM] * len(arrays),
        out_specs=specs[0] if single else specs,
        scratch_shapes=list(scratch),
        input_output_aliases=aliases or {},
        compiler_params=params(mib),
        name=name,
    )(*scalars, *[near(a) for a in arrays])


def on_device(exit_grad, stored_waves, object_slices, propagator_taps, positions, counts):
    slices, cap, side = stored_waves.shape[:3]
    rows = object_slices.shape[1]
    groups = lax.axis_size("depth")
    tiles = lax.axis_size("tile")
    group_index = lax.axis_index("depth")
    at = jnp.stack([group_index, lax.axis_index("tile")])
    spots = positions.T
    up = [(i, (i + 1) % tiles) for i in range(tiles)]
    down = [(i, (i - 1) % tiles) for i in range(tiles)]

    received_exits = [lax.ppermute(exit_grad, "depth", [(g, groups - 1)]) for g in range(groups - 1)]
    exits = [as_rows(e) for e in received_exits + [exit_grad]]
    obj = near(as_rows(object_slices))

    edge_shape = pltpu.VMEM((slices, 2, rows, LANES), BF16)
    left_edge, right_edge, my_count = kernel_call(
        edges_kernel, (at, counts), (obj,), (edge_shape, edge_shape, pltpu.SMEM((1,), jnp.int32)), name="edges"
    )
    from_left = lax.ppermute(right_edge, "tile", up)
    from_right = lax.ppermute(left_edge, "tile", down)

    wide_scratch = pltpu.VMEM((2 * side * 4, LANES), F32)
    rhs_scratch = pltpu.VMEM((2 * side, 2 * side), BF16)
    h_scratch = pltpu.VMEM((side, 2 * side), F32)
    wave_shape = pltpu.VMEM((side, 2 * side), BF16)

    planes, col_mats, row_mats = kernel_call(
        setup_kernel,
        (at, spots, counts, propagator_taps),
        (as_rows(stored_waves),),
        (
            pltpu.VMEM((cap, slices, 2, side, side), BF16),
            pltpu.VMEM((cap, 2 * side, 2 * side), BF16),
            pltpu.VMEM((cap, side, 2 * side), BF16),
        ),
        (pltpu.VMEM((4, 3, LANES, LANES), F32), wide_scratch),
        name="setup",
    )
    shared = (obj, from_left, from_right, col_mats, row_mats)

    def forward(j, group, incoming):
        return kernel_call(
            functools.partial(forward_kernel, j, group, group == groups - 1, len(incoming)),
            (at, spots),
            (*shared, *incoming),
            wave_shape,
            (wide_scratch, rhs_scratch, h_scratch),
            name=f"forward{j}",
        )

    def gradient(j, received, sums):
        old = () if sums is None else (sums,)
        return kernel_call(
            functools.partial(grad_kernel, groups, j, sums is None, len(exits)),
            (at, spots),
            (*shared, planes, received, *exits, *old),
            pltpu.VMEM((slices, 2, 4, rows, LANES), F32),
            (wide_scratch, wave_shape, rhs_scratch, h_scratch),
            {} if sums is None else {9 + len(exits): 0},
            name=f"gradient{j}",
        )

    def with_live(live):
        def run():
            waves = [exits] * live
            received = [None] * live
            for group in range(groups - 1, 0, -1):
                for j in range(live):
                    incoming = waves[j] if group == groups - 1 else [waves[j]]
                    sent = forward(j, group, incoming)
                    arrived = lax.ppermute(sent, "depth", [(group, group - 1)])
                    waves[j] = arrived
                    mine = group_index == group - 1
                    received[j] = arrived if received[j] is None else jnp.where(mine, arrived, received[j])
            sums = None
            for j in range(live):
                wave = jnp.zeros((side, 2 * side), BF16) if received[j] is None else received[j]
                sums = gradient(j, wave, sums)
            own_shape = pltpu.VMEM((slices, 2, 2, rows, LANES), BF16)
            return kernel_call(rims_kernel, (), (sums,), (edge_shape, edge_shape, own_shape), name="rims")

        return run

    left_rim, right_rim, own = lax.switch(my_count[0] - 1, [with_live(n + 1) for n in range(cap)])
    sums_left = lax.ppermute(right_rim, "tile", up)
    sums_right = lax.ppermute(left_rim, "tile", down)
    out_rows = pl.pallas_call(
        close_kernel,
        out_shape=jax.ShapeDtypeStruct((slices * rows * 4, LANES), BF16),
        in_specs=[VMEM, VMEM, VMEM],
        out_specs=VMEM,
        scratch_shapes=[pltpu.VMEM((slices * rows * 4, LANES), F32)],
        compiler_params=params(16),
        name="close",
    )(near(own), near(sums_left), near(sums_right))
    return from_rows(out_rows, (slices, rows, 2, 2 * LANES))


def solution(mesh):
    return jax.shard_map(
        on_device,
        mesh=mesh,
        in_specs=(
            P("tile", "depth", None, None),
            P("depth", "tile", None, None, None),
            P("depth", None, None, "tile"),
            P(),
            P(),
            P(),
        ),
        out_specs=P("depth", None, None, "tile"),
        check_vma=False,
    )
```

```python
import functools

import jax
import jax.numpy as jnp
from jax import lax
from jax.experimental import pallas as pl
from jax.experimental.pallas import tpu as pltpu
from jax.sharding import PartitionSpec as P

LANES = 128
CHUNK = 64
STEP = 32
F32 = jnp.float32
BF16 = jnp.bfloat16
VMEM = pl.BlockSpec(memory_space=pltpu.VMEM)
SMEM = pl.BlockSpec(memory_space=pltpu.SMEM)
HBM = pl.BlockSpec(memory_space=pltpu.HBM)


def as_rows(x):
    *lead, parts, columns = x.shape
    tiles = columns // LANES
    split = x.reshape(*lead, parts, tiles, LANES)
    return jnp.swapaxes(split, -3, -2).reshape(-1, LANES)


def from_rows(x, shape):
    *lead, parts, columns = shape
    tiles = columns // LANES
    split = x.reshape(*lead, tiles, parts, LANES)
    return jnp.swapaxes(split, -3, -2).reshape(shape)


def row_ids(start, rows):
    return lax.broadcasted_iota(jnp.int32, (rows, LANES), 0) + start


def lane_ids(rows):
    return lax.broadcasted_iota(jnp.int32, (rows, LANES), 1)


class Place:
    def __init__(self, info, j, cap):
        self.row = info[3 + j]
        self.col = info[3 + cap + j]
        self.mixed = jnp.where(self.col < LANES, 0, 1)

    def on_halo(self, rows):
        column = lane_ids(rows) + self.mixed * LANES
        return (column >= self.col) == (self.mixed == 0)


def first_kernel(
    counts, positions, taps, obj_in, left_edge, right_edge, info, taps_out, obj, counts_in, spots, small_sem, obj_sem
):
    slices, parts, rows, _ = left_edge.shape
    cap = (info.shape[0] - 3) // 2
    small = [
        pltpu.make_async_copy(source, target, small_sem.at[i])
        for i, (source, target) in enumerate(((counts, counts_in), (positions, spots), (taps, taps_out)))
    ]
    length = rows * 4
    loads = [
        pltpu.make_async_copy(obj_in.at[pl.ds(s * length, length)], obj.at[pl.ds(s * length, length)], obj_sem.at[s])
        for s in range(slices)
    ]
    for copy in loads + small:
        copy.start()
    for s in range(slices):
        loads[s].wait()
        for c in range(parts):
            left_edge[s, c] = obj[pl.ds(s * length + c, rows, stride=4), :].astype(BF16)
            right_edge[s, c] = obj[pl.ds(s * length + 2 + c, rows, stride=4), :].astype(BF16)
    for copy in small:
        copy.wait()
    tile = lax.axis_index("tile")
    info[0] = lax.axis_index("depth")
    info[1] = tile
    info[2] = counts_in[tile]
    for j in range(cap):
        info[3 + j] = spots[0, tile * cap + j]
        info[3 + cap + j] = spots[1, tile * cap + j]


def build_blocks(taps, blocks):
    tap_count = taps.shape[2]
    centre = tap_count // 2

    def tap(m, k):
        return taps[1, m, k] if m < 2 else taps[0, m - 2, tap_count - 1 - k]

    def build(block, first, shift, ks):
        diff = lane_ids(STEP) - row_ids(first, STEP) + shift
        total = [jnp.zeros((STEP, LANES), F32) for _ in range(4)]
        for k in ks:
            hit = diff == k - centre
            for m in range(4):
                total[m] = jnp.where(hit, tap(m, k), total[m])
        for m in range(4):
            blocks[m, block, pl.ds(first, STEP), :] = total[m]

    def diagonal(i, carry):
        build(0, pl.multiple_of(i * STEP, STEP), 0, range(tap_count))
        return carry

    lax.fori_loop(0, LANES // STEP, diagonal, 0)
    for first in range(0, LANES, STEP):
        build(1, first, LANES, range(centre + 1, tap_count) if first + STEP == LANES else ())
        build(2, first, -LANES, range(centre) if first == 0 else ())


def matrices_kernel(info, taps, col_mat, row_mat, blocks):
    cap = col_mat.shape[0]
    side = row_mat.shape[0]
    build_blocks(taps, blocks)

    def rows_of(i, tile_row):
        return pl.ds(pl.multiple_of(i * STEP + tile_row * LANES, STEP), STEP)

    def low_rows_of(i, tile_row):
        return pl.ds(pl.multiple_of(i * STEP + tile_row * LANES + side, STEP), STEP)

    def row_part(i, carry):
        for tr in range(2):
            for tc in range(2):
                block = 0 if tr == tc else 1 + tr
                for c in range(2):
                    value = blocks[2 + c, block, pl.ds(pl.multiple_of(i * STEP, STEP), STEP), :]
                    row_mat[rows_of(i, tr), pl.ds(tc * LANES + c * side, LANES)] = value.astype(BF16)
        return carry

    lax.fori_loop(0, LANES // STEP, row_part, 0)

    def slot(j, carry):
        seam = Place(info, j, cap).col

        def fill(i, inner):
            first = pl.multiple_of(i * STEP, STEP)
            for tr in range(2):
                for tc in range(2):
                    row_side = row_ids(first, STEP) + tr * LANES >= seam
                    col_side = lane_ids(STEP) + tc * LANES >= seam
                    same = row_side == col_side
                    values = []
                    for m in range(2):
                        if tr == tc:
                            close, far = blocks[m, 0, pl.ds(first, STEP), :], 0.0
                        else:
                            close = blocks[m, 1 + tr, pl.ds(first, STEP), :]
                            far = blocks[m, 2 - tr, pl.ds(first, STEP), :]
                        values.append(jnp.where(same, close, far))
                    re, im = values[0].astype(BF16), values[1].astype(BF16)
                    re_cols = pl.ds(tc * LANES, LANES)
                    im_cols = pl.ds(tc * LANES + side, LANES)
                    col_mat[j, rows_of(i, tr), re_cols] = re
                    col_mat[j, rows_of(i, tr), im_cols] = -im
                    col_mat[j, low_rows_of(i, tr), re_cols] = im
                    col_mat[j, low_rows_of(i, tr), im_cols] = re
            return inner

        return lax.fori_loop(0, LANES // STEP, fill, carry)

    lax.fori_loop(0, info[2], slot, 0)


def halo_kernel(from_left, from_right, halos):
    halos[0] = from_left[...].astype(F32)
    halos[1] = from_right[...].astype(F32)


def unpack(place, sources, wide, write):
    side = 0
    for ref, start, count in sources:
        wide[pl.ds(side * 4, count * 4), :] = ref[pl.ds(start, count * 4), :].astype(F32)
        side += count

    def move(i, carry):
        a = pl.multiple_of(i * CHUNK, CHUNK)
        for c in range(2):
            halves = [wide[pl.ds(a * 4 + ct * 2 + c, CHUNK, stride=4), :] for ct in range(2)]
            value = pltpu.roll(jnp.concatenate(halves, axis=1), place.col, 1)
            write(c, pl.ds(a, CHUNK), value.astype(BF16))
        return carry

    lax.fori_loop(0, side // CHUNK, move, 0)


def stored_kernel(info, stored, planes, own_sums, halo_sums, wide):
    live, slices, _, side, _ = planes.shape
    cap = (info.shape[0] - 3) // 2
    own_sums[...] = jnp.zeros(own_sums.shape, F32)
    halo_sums[...] = jnp.zeros(halo_sums.shape, F32)

    def one(i, carry):
        j = i // slices
        s = i % slices

        def write(c, rows, value):
            planes[j, s, c, rows] = value

        start = pl.multiple_of((s * cap + j) * side * 4, side * 4)
        unpack(Place(info, j, cap), [(stored, start, side)], wide, write)
        return carry

    lax.fori_loop(0, live * slices, one, 0)


def back(j, wave, col_mat, row_mat, rhs, h_buf, s):
    side = wave.shape[0]
    mixed = jnp.dot(wave[...], col_mat[j], preferred_element_type=F32).astype(BF16)
    rhs[:side, :] = mixed
    rhs[side:, :side] = mixed[:, side:]
    rhs[side:, side:] = -mixed[:, :side]
    h_buf[s] = jnp.dot(row_mat[...], rhs[...], preferred_element_type=F32)


def tile_columns(ct, c, side):
    return pl.ds(pl.multiple_of(ct * LANES + c * side, LANES), LANES)


def leave(place, s, a, obj, halos, h_buf, wave, total_rows):
    side = wave.shape[0]
    rows = pl.ds(a, CHUNK)
    on_halo = place.on_halo(CHUNK)
    for ct, own in ((place.mixed, 1 - place.mixed), (1 - place.mixed, place.mixed)):
        o = []
        for c in range(2):
            first = (s * total_rows + place.row + a) * 4 + own * 2 + c
            value = obj[pl.ds(first, CHUNK, stride=4), :]
            if ct is place.mixed:
                beyond = halos[place.mixed, s, c, pl.ds(place.row + a, CHUNK), :]
                value = jnp.where(on_halo, beyond, value)
            o.append(value)
        h_re = h_buf[s, rows, tile_columns(ct, 0, side)]
        h_im = h_buf[s, rows, tile_columns(ct, 1, side)]
        wave[rows, tile_columns(ct, 0, side)] = (o[0] * h_re + o[1] * h_im).astype(BF16)
        wave[rows, tile_columns(ct, 1, side)] = (o[0] * h_im - o[1] * h_re).astype(BF16)


def collect(place, j, s, a, planes, h_buf, own_sums, halo_sums):
    side = h_buf.shape[1]
    rows = pl.ds(a, CHUNK)
    frame_rows = pl.ds(place.row + a, CHUNK)
    on_halo = place.on_halo(CHUNK)
    for ct, own in ((place.mixed, 1 - place.mixed), (1 - place.mixed, place.mixed)):
        cols = tile_columns(ct, 0, side)
        st_re = planes[j, s, 0, rows, cols].astype(F32)
        st_im = planes[j, s, 1, rows, cols].astype(F32)
        h_re = h_buf[s, rows, cols]
        h_im = h_buf[s, rows, tile_columns(ct, 1, side)]
        for c, g in enumerate((st_re * h_re + st_im * h_im, st_re * h_im - st_im * h_re)):
            if ct is place.mixed:
                halo_sums[place.mixed, s, c, frame_rows, :] += jnp.where(on_halo, g, 0.0)
                own_sums[own, s, c, frame_rows, :] += jnp.where(on_halo, 0.0, g)
            else:
                own_sums[own, s, c, frame_rows, :] += g


def each_chunk(side, body):
    def step(k, carry):
        body(pl.multiple_of(k * CHUNK, CHUNK))
        return carry

    lax.fori_loop(0, side // CHUNK, step, 0)


def each_slice(slices, body):
    def step(i, carry):
        body(slices - 1 - i)
        return carry

    lax.fori_loop(0, slices, step, 0)


def forward_kernel(j, group, last, n_in, *refs):
    info, obj, halos, col_mat, row_mat = refs[:5]
    incoming = refs[5 : 5 + n_in]
    out, h_buf, wide, rhs = refs[5 + n_in :]
    slices, side = h_buf.shape[:2]
    total_rows = halos.shape[3]

    @pl.when(info[0] == group)
    def _():
        place = Place(info, j, col_mat.shape[0])
        if last:
            count = side // n_in

            def write(c, rows, value):
                out[rows, pl.ds(c * side, side)] = value

            unpack(place, [(ref, j * count * 4, count) for ref in incoming], wide, write)
        else:
            out[...] = incoming[0][...]

        def one_slice(s):
            back(j, out, col_mat, row_mat, rhs, h_buf, s)
            each_chunk(side, lambda a: leave(place, s, a, obj, halos, h_buf, out, total_rows))

        each_slice(slices, one_slice)


def grad_kernel(groups, j, *refs):
    info, obj, halos, col_mat, row_mat, planes, received, h_last, _, _ = refs[:10]
    own_sums, halo_sums, wave, rhs, h_buf = refs[10:]
    slices, side = h_last.shape[:2]
    total_rows = halos.shape[3]
    place = Place(info, j, col_mat.shape[0])

    @pl.when(info[0] == groups - 1)
    def _():
        each_slice(
            slices,
            lambda s: each_chunk(side, lambda a: collect(place, j, s, a, planes, h_last, own_sums, halo_sums)),
        )

    @pl.when(info[0] != groups - 1)
    def _():
        wave[...] = received[...]

        def one_slice(s):
            back(j, wave, col_mat, row_mat, rhs, h_buf, s)

            @pl.when(s > 0)
            def _():
                each_chunk(side, lambda a: leave(place, s, a, obj, halos, h_buf, wave, total_rows))

            each_chunk(side, lambda a: collect(place, j, s, a, planes, h_buf, own_sums, halo_sums))

        each_slice(slices, one_slice)


def rims_kernel(own_sums, halo_sums, left_rim, right_rim, own):
    left_rim[...] = halo_sums[0].astype(BF16)
    right_rim[...] = halo_sums[1].astype(BF16)
    own[...] = own_sums[...].astype(BF16)


def close_kernel(own, from_left, from_right, out, mix):
    _, slices, parts, rows, _ = own.shape
    for s in range(slices):
        for c in range(parts):
            for ct, other in ((0, from_left), (1, from_right)):
                total = own[ct, s, c].astype(F32) + other[s, c].astype(F32)
                mix[pl.ds(s * rows * 4 + ct * 2 + c, rows, stride=4), :] = total
    out[...] = mix[...].astype(BF16)


def near(x):
    return pltpu.with_memory_space_constraint(x, pltpu.VMEM)


def far(x):
    return pltpu.with_memory_space_constraint(x, pltpu.HBM)


def kernel_call(body, scalars, arrays, out, scratch=(), aliases=None, mib=8, name=None):
    single = not isinstance(out, tuple)
    specs = tuple(SMEM if o.memory_space == pltpu.SMEM else VMEM for o in ((out,) if single else out))
    return pl.pallas_call(
        body,
        out_shape=out,
        in_specs=[SMEM] * len(scalars) + [VMEM] * len(arrays),
        out_specs=specs[0] if single else specs,
        scratch_shapes=list(scratch),
        input_output_aliases=aliases or {},
        compiler_params=pltpu.CompilerParams(vmem_limit_bytes=mib << 20),
        name=name,
    )(*scalars, *[near(a) for a in arrays])


def on_device(exit_grad, stored_waves, object_slices, propagator_taps, positions, counts):
    slices, cap, side = stored_waves.shape[:3]
    rows = object_slices.shape[1]
    groups = lax.axis_size("depth")
    tiles = lax.axis_size("tile")
    group_index = lax.axis_index("depth")
    up = [(i, (i + 1) % tiles) for i in range(tiles)]
    down = [(i, (i - 1) % tiles) for i in range(tiles)]

    received_exits = [lax.ppermute(exit_grad, "depth", [(g, groups - 1)]) for g in range(groups - 1)]
    exits = [as_rows(e) for e in received_exits + [exit_grad]]

    edge_shape = pltpu.VMEM((slices, 2, rows, LANES), BF16)
    spots = positions.T
    left_edge, right_edge, info, taps, obj = pl.pallas_call(
        first_kernel,
        out_shape=(
            edge_shape,
            edge_shape,
            pltpu.SMEM((3 + 2 * cap,), jnp.int32),
            pltpu.SMEM(propagator_taps.shape, F32),
            pltpu.VMEM((slices * rows * 4, LANES), F32),
        ),
        in_specs=[HBM] * 4,
        out_specs=(VMEM, VMEM, SMEM, SMEM, VMEM),
        scratch_shapes=[
            pltpu.SMEM(counts.shape, jnp.int32),
            pltpu.SMEM(spots.shape, jnp.int32),
            pltpu.SemaphoreType.DMA((3,)),
            pltpu.SemaphoreType.DMA((slices,)),
        ],
        compiler_params=pltpu.CompilerParams(vmem_limit_bytes=8 << 20),
        name="first",
    )(*[far(a) for a in (counts, spots, propagator_taps, as_rows(object_slices))])
    from_left = lax.ppermute(right_edge, "tile", up)
    from_right = lax.ppermute(left_edge, "tile", down)

    col_mats, row_mat = kernel_call(
        matrices_kernel,
        (info, taps),
        (),
        (pltpu.VMEM((cap, 2 * side, 2 * side), BF16), pltpu.VMEM((side, 2 * side), BF16)),
        (pltpu.VMEM((4, 3, LANES, LANES), F32),),
        name="matrices",
    )
    halos = kernel_call(
        halo_kernel, (), (from_left, from_right), pltpu.VMEM((2, slices, 2, rows, LANES), F32), name="halos"
    )
    shared = (obj, halos, col_mats, row_mat)
    stored = as_rows(stored_waves)

    wide_scratch = pltpu.VMEM((side * 4, LANES), F32)
    rhs_scratch = pltpu.VMEM((2 * side, 2 * side), BF16)
    wave_shape = pltpu.VMEM((side, 2 * side), BF16)
    h_shape = pltpu.VMEM((slices, side, 2 * side), F32)
    sums_shape = pltpu.VMEM((2, slices, 2, rows, LANES), F32)

    def forward(j, group, incoming):
        return kernel_call(
            functools.partial(forward_kernel, j, group, group == groups - 1, len(incoming)),
            (info,),
            (*shared, *incoming),
            (wave_shape, h_shape),
            (wide_scratch, rhs_scratch),
            name=f"forward{j}",
        )

    def gradient(j, planes, received, h_last, sums):
        return kernel_call(
            functools.partial(grad_kernel, groups, j),
            (info,),
            (*shared, planes, received, h_last, *sums),
            (sums_shape, sums_shape),
            (wave_shape, rhs_scratch, h_shape),
            {8: 0, 9: 1},
            name=f"gradient{j}",
        )

    def with_live(live):
        def run():
            waves = [exits] * live
            received = [None] * live
            h_last = [None] * live
            for group in range(groups - 1, 0, -1):
                for j in range(live):
                    last = group == groups - 1
                    sent, h = forward(j, group, waves[j] if last else [waves[j]])
                    if last:
                        h_last[j] = h
                    arrived = lax.ppermute(sent, "depth", [(group, group - 1)])
                    waves[j] = arrived
                    mine = group_index == group - 1
                    received[j] = arrived if last else jnp.where(mine, arrived, received[j])
            planes, *sums = kernel_call(
                stored_kernel,
                (info,),
                (stored,),
                (pltpu.VMEM((live, slices, 2, side, side), BF16), sums_shape, sums_shape),
                (wide_scratch,),
                name="stored",
            )
            for j in range(live):
                sums = gradient(j, planes, received[j], h_last[j], sums)
            own_shape = pltpu.VMEM((2, slices, 2, rows, LANES), BF16)
            return kernel_call(rims_kernel, (), sums, (edge_shape, edge_shape, own_shape), name="rims")

        return run

    left_rim, right_rim, own = lax.switch(info[2] - 1, [with_live(n + 1) for n in range(cap)])
    sums_left = lax.ppermute(right_rim, "tile", up)
    sums_right = lax.ppermute(left_rim, "tile", down)
    out_rows = pl.pallas_call(
        close_kernel,
        out_shape=jax.ShapeDtypeStruct((slices * rows * 4, LANES), BF16),
        in_specs=[VMEM, VMEM, VMEM],
        out_specs=VMEM,
        scratch_shapes=[pltpu.VMEM((slices * rows * 4, LANES), F32)],
        compiler_params=pltpu.CompilerParams(vmem_limit_bytes=16 << 20),
        name="close",
    )(near(own), near(sums_left), near(sums_right))
    return from_rows(out_rows, (slices, rows, 2, 2 * LANES))


def solution(mesh):
    return jax.shard_map(
        on_device,
        mesh=mesh,
        in_specs=(
            P("tile", "depth", None, None),
            P("depth", "tile", None, None, None),
            P("depth", None, None, "tile"),
            P(),
            P(),
            P(),
        ),
        out_specs=P("depth", None, None, "tile"),
        check_vma=False,
    )
```

```python
import functools

import jax
import jax.numpy as jnp
from jax import lax
from jax.experimental import pallas as pl
from jax.experimental.pallas import tpu as pltpu
from jax.sharding import PartitionSpec as P


LANES = 128
CHUNK = 64
STEP = 32
PACKED = 16
F32 = jnp.float32
BF16 = jnp.bfloat16
VMEM = pl.BlockSpec(memory_space=pltpu.VMEM)
SMEM = pl.BlockSpec(memory_space=pltpu.SMEM)
HBM = pl.BlockSpec(memory_space=pltpu.HBM)


def as_rows(x):
    *lead, parts, columns = x.shape
    tiles = columns // LANES
    split = x.reshape(*lead, parts, tiles, LANES)
    return jnp.swapaxes(split, -3, -2).reshape(-1, LANES)


def from_rows(x, shape):
    *lead, parts, columns = shape
    tiles = columns // LANES
    split = x.reshape(*lead, tiles, parts, LANES)
    return jnp.swapaxes(split, -3, -2).reshape(shape)


def row_ids(start, rows):
    return lax.broadcasted_iota(jnp.int32, (rows, LANES), 0) + start


def lane_ids(rows):
    return lax.broadcasted_iota(jnp.int32, (rows, LANES), 1)


class Place:
    def __init__(self, info, j, cap):
        self.row = info[3 + j]
        self.col = info[3 + cap + j]
        self.mixed = jnp.where(self.col < LANES, 0, 1)

    def halo_first(self, total_rows, halo_rows):
        return pl.multiple_of(jnp.minimum(self.row // PACKED * PACKED, total_rows - halo_rows), PACKED)

    def on_halo(self, rows):
        column = lane_ids(rows) + self.mixed * LANES
        return (column >= self.col) == (self.mixed == 0)


def first_kernel(
    counts,
    positions,
    taps,
    obj_in,
    cross_edge,
    chip_edge,
    info,
    taps_out,
    obj,
    counts_in,
    spots,
    small_sem,
    obj_sem,
):
    cap = (info.shape[0] - 3) // 2
    slices, parts, rows, _ = cross_edge.shape
    pieces = obj_sem.shape[0]
    piece_rows = slices * rows // pieces

    def copy(source, target, sem):
        return pltpu.make_async_copy(source, target, sem)

    small = [
        copy(source, target, small_sem.at[i])
        for i, (source, target) in enumerate(((counts, counts_in), (positions, spots), (taps, taps_out)))
    ]
    loads = []
    for p in range(pieces):
        part = pl.ds(p * piece_rows * 4, piece_rows * 4)
        loads.append(copy(obj_in.at[part], obj.at[part], obj_sem.at[p]))
    for each in loads + small:
        each.start()
    tile = lax.axis_index("tile")
    cross_side = tile % 2
    for p in range(pieces):
        loads[p].wait()
        s, first = divmod(p * piece_rows, rows)
        start = p * piece_rows * 4
        for c in range(parts):
            beyond = obj[pl.ds(start + cross_side * 2 + c, piece_rows, stride=4), :]
            beside = obj[pl.ds(start + (1 - cross_side) * 2 + c, piece_rows, stride=4), :]
            cross_edge[s, c, pl.ds(first, piece_rows), :] = beyond.astype(BF16)
            chip_edge[s, c, pl.ds(first, piece_rows), :] = beside.astype(BF16)
    for each in small:
        each.wait()
    info[0] = lax.axis_index("depth")
    info[1] = tile
    info[2] = counts_in[tile]
    for j in range(cap):
        info[3 + j] = spots[0, tile * cap + j]
        info[3 + cap + j] = spots[1, tile * cap + j]


def build_blocks(taps, blocks):
    tap_count = taps.shape[2]
    centre = tap_count // 2

    def tap(m, k):
        return taps[1, m, k] if m < 2 else taps[0, m - 2, tap_count - 1 - k]

    def build(block, first, shift, ks):
        diff = lane_ids(STEP) - row_ids(first, STEP) + shift
        total = [jnp.zeros((STEP, LANES), F32) for _ in range(4)]
        for k in ks:
            hit = diff == k - centre
            for m in range(4):
                total[m] = jnp.where(hit, tap(m, k), total[m])
        for m in range(4):
            blocks[m, block, pl.ds(first, STEP), :] = total[m]

    def diagonal(i, carry):
        build(0, pl.multiple_of(i * STEP, STEP), 0, range(tap_count))
        return carry

    lax.fori_loop(0, LANES // STEP, diagonal, 0)
    for first in range(0, LANES, STEP):
        build(1, first, LANES, range(centre + 1, tap_count) if first + STEP == LANES else ())
        build(2, first, -LANES, range(centre) if first == 0 else ())


def matrices_kernel(info, taps, col_mat, row_mat, blocks):
    cap = col_mat.shape[0]
    side = row_mat.shape[0]
    build_blocks(taps, blocks)

    def rows_of(i, tile_row):
        return pl.ds(pl.multiple_of(i * STEP + tile_row * LANES, STEP), STEP)

    def low_rows_of(i, tile_row):
        return pl.ds(pl.multiple_of(i * STEP + tile_row * LANES + side, STEP), STEP)

    def row_part(i, carry):
        for tr in range(2):
            for tc in range(2):
                block = 0 if tr == tc else 1 + tr
                for c in range(2):
                    value = blocks[2 + c, block, pl.ds(pl.multiple_of(i * STEP, STEP), STEP), :]
                    row_mat[rows_of(i, tr), pl.ds(tc * LANES + c * side, LANES)] = value.astype(BF16)
        return carry

    lax.fori_loop(0, LANES // STEP, row_part, 0)

    def slot(j, carry):
        seam = Place(info, j, cap).col

        def fill(i, inner):
            first = pl.multiple_of(i * STEP, STEP)
            for tr in range(2):
                for tc in range(2):
                    row_side = row_ids(first, STEP) + tr * LANES >= seam
                    col_side = lane_ids(STEP) + tc * LANES >= seam
                    same = row_side == col_side
                    values = []
                    for m in range(2):
                        if tr == tc:
                            close, far = blocks[m, 0, pl.ds(first, STEP), :], 0.0
                        else:
                            close = blocks[m, 1 + tr, pl.ds(first, STEP), :]
                            far = blocks[m, 2 - tr, pl.ds(first, STEP), :]
                        values.append(jnp.where(same, close, far))
                    re, im = values[0].astype(BF16), values[1].astype(BF16)
                    re_cols = pl.ds(tc * LANES, LANES)
                    im_cols = pl.ds(tc * LANES + side, LANES)
                    col_mat[j, rows_of(i, tr), re_cols] = re
                    col_mat[j, rows_of(i, tr), im_cols] = -im
                    col_mat[j, low_rows_of(i, tr), re_cols] = im
                    col_mat[j, low_rows_of(i, tr), im_cols] = re
            return inner

        return lax.fori_loop(0, LANES // STEP, fill, carry)

    lax.fori_loop(0, info[2], slot, 0)


def take_halo(info, place, across, inside, halo):
    rows = pl.ds(place.halo_first(across.shape[2], halo.shape[2]), halo.shape[2])
    from_across = place.mixed == info[1] % 2

    @pl.when(from_across)
    def _():
        halo[...] = across[:, :, rows, :].astype(F32)

    @pl.when(jnp.logical_not(from_across))
    def _():
        halo[...] = inside[:, :, rows, :].astype(F32)


def unpack(place, sources, wide, write):
    side = 0
    for packed, start, count in sources:
        wide[pl.ds(side * 4, count * 4), :] = packed[pl.ds(start, count * 4), :].astype(F32)
        side += count

    def move(i, carry):
        a = pl.multiple_of(i * CHUNK, CHUNK)
        for c in range(2):
            halves = [wide[pl.ds(a * 4 + ct * 2 + c, CHUNK, stride=4), :] for ct in range(2)]
            value = pltpu.roll(jnp.concatenate(halves, axis=1), place.col, 1)
            write(c, pl.ds(a, CHUNK), value.astype(BF16))
        return carry

    lax.fori_loop(0, side // CHUNK, move, 0)


def unpack_stored(place, j, cap, stored, planes, packed, sems, wide):
    slices, _, side, _ = planes.shape

    def load(s):
        start = pl.multiple_of((s * cap + j) * side * 4, side * 4)
        return pltpu.make_async_copy(stored.at[pl.ds(start, side * 4)], packed.at[s], sems.at[s])

    def begin(s, carry):
        load(s).start()
        return carry

    def one(s, carry):
        def write(c, rows, value):
            planes[s, c, rows] = value

        load(s).wait()
        unpack(place, [(packed.at[s], 0, side)], wide, write)
        return carry

    lax.fori_loop(0, slices, begin, 0)
    lax.fori_loop(0, slices, one, 0)


def back(j, wave, col_mat, row_mat, rhs, h_buf, s):
    side = wave.shape[0]
    mixed = jnp.dot(wave[...], col_mat[j], preferred_element_type=F32).astype(BF16)
    rhs[:side, :] = mixed
    rhs[side:, :side] = mixed[:, side:]
    rhs[side:, side:] = -mixed[:, :side]
    h_buf[s] = jnp.dot(row_mat[...], rhs[...], preferred_element_type=F32)


def tile_columns(ct, c, side):
    return pl.ds(pl.multiple_of(ct * LANES + c * side, LANES), LANES)


def leave(place, s, a, obj, halo, h_buf, wave):
    side = wave.shape[0]
    total_rows = obj.shape[0] // h_buf.shape[0] // 4
    halo_row = place.row - place.halo_first(total_rows, halo.shape[2]) + a
    rows = pl.ds(a, CHUNK)
    on_halo = place.on_halo(CHUNK)
    for ct, own in ((place.mixed, 1 - place.mixed), (1 - place.mixed, place.mixed)):
        o = []
        for c in range(2):
            first = (s * total_rows + place.row + a) * 4 + own * 2 + c
            value = obj[pl.ds(first, CHUNK, stride=4), :]
            if ct is place.mixed:
                beyond = halo[s, c, pl.ds(halo_row, CHUNK), :]
                value = jnp.where(on_halo, beyond, value)
            o.append(value)
        h_re = h_buf[s, rows, tile_columns(ct, 0, side)]
        h_im = h_buf[s, rows, tile_columns(ct, 1, side)]
        wave[rows, tile_columns(ct, 0, side)] = (o[0] * h_re + o[1] * h_im).astype(BF16)
        wave[rows, tile_columns(ct, 1, side)] = (o[0] * h_im - o[1] * h_re).astype(BF16)


def collect(place, s, a, planes, h_buf, own_sums, halo_sums):
    side = h_buf.shape[1]
    rows = pl.ds(a, CHUNK)
    frame_rows = pl.ds(place.row + a, CHUNK)
    on_halo = place.on_halo(CHUNK)
    for ct, own in ((place.mixed, 1 - place.mixed), (1 - place.mixed, place.mixed)):
        cols = tile_columns(ct, 0, side)
        st_re = planes[s, 0, rows, cols].astype(F32)
        st_im = planes[s, 1, rows, cols].astype(F32)
        h_re = h_buf[s, rows, cols]
        h_im = h_buf[s, rows, tile_columns(ct, 1, side)]
        for c, g in enumerate((st_re * h_re + st_im * h_im, st_re * h_im - st_im * h_re)):
            if ct is place.mixed:
                halo_sums[place.mixed, s, c, frame_rows, :] += jnp.where(on_halo, g, 0.0)
                own_sums[own, s, c, frame_rows, :] += jnp.where(on_halo, 0.0, g)
            else:
                own_sums[own, s, c, frame_rows, :] += g


def each_chunk(side, body):
    def step(k, carry):
        body(pl.multiple_of(k * CHUNK, CHUNK))
        return carry

    lax.fori_loop(0, side // CHUNK, step, 0)


def each_slice(slices, body):
    def step(i, carry):
        body(slices - 1 - i)
        return carry

    lax.fori_loop(0, slices, step, 0)


def take_exit(place, j, incoming, out, wide):
    side = out.shape[0]
    count = side // len(incoming)

    def write(c, rows, value):
        out[rows, pl.ds(c * side, side)] = value

    unpack(place, [(ref, j * count * 4, count) for ref in incoming], wide, write)


def start_kernel(groups, n_in, *refs):
    info, col_mat, row_mat = refs[:3]
    incoming = refs[3 : 3 + n_in]
    h_buf, out, wide, rhs = refs[3 + n_in :]
    place = Place(info, 0, col_mat.shape[0])

    @pl.when(info[0] == groups - 1)
    def _():
        take_exit(place, 0, incoming, out, wide)
        back(0, out, col_mat, row_mat, rhs, h_buf, 0)


def resume_kernel(
    groups,
    info,
    stored,
    obj,
    across,
    inside,
    col_mat,
    row_mat,
    old_h,
    out,
    h_buf,
    planes,
    halo,
    rhs,
    wide,
    packed,
    sems,
):
    slices, side = h_buf.shape[:2]
    place = Place(info, 0, col_mat.shape[0])
    take_halo(info, place, across, inside, halo)

    @pl.when(info[0] == groups - 1)
    def _():
        h_buf[slices - 1] = old_h[0]

        def one_slice(s):
            each_chunk(side, lambda a: leave(place, s, a, obj, halo, h_buf, out))

            @pl.when(s > 0)
            def _():
                back(0, out, col_mat, row_mat, rhs, h_buf, s - 1)

        each_slice(slices, one_slice)

    @pl.when(info[0] != groups - 1)
    def _():
        unpack_stored(place, 0, col_mat.shape[0], stored, planes, packed, sems, wide)


def forward_kernel(groups, j, group, n_in, *refs):
    info, stored, obj, across, inside, col_mat, row_mat = refs[:7]
    incoming = refs[7 : 7 + n_in]
    out, h_buf, planes, halo, wide, rhs, packed, sems = refs[7 + n_in :]
    slices, side = h_buf.shape[:2]
    cap = col_mat.shape[0]
    last = group == groups - 1
    place = Place(info, j, cap)
    take_halo(info, place, across, inside, halo)

    @pl.when(info[0] == group)
    def _():
        if last:
            take_exit(place, j, incoming, out, wide)
        else:
            out[...] = incoming[0][...]

        def one_slice(s):
            back(j, out, col_mat, row_mat, rhs, h_buf, s)
            each_chunk(side, lambda a: leave(place, s, a, obj, halo, h_buf, out))

        each_slice(slices, one_slice)

    if last:

        @pl.when(info[0] != group)
        def _():
            unpack_stored(place, j, cap, stored, planes, packed, sems, wide)


def grad_kernel(groups, j, *refs):
    info, stored, obj, col_mat, row_mat, halo, planes_in, received, h_last = refs[:9]
    own_sums, halo_sums, wave, rhs, h_buf, planes, wide, packed, sems = refs[-9:]
    slices, side = h_last.shape[:2]
    cap = col_mat.shape[0]
    place = Place(info, j, cap)
    if j == 0:
        own_sums[...] = jnp.zeros(own_sums.shape, F32)
        halo_sums[...] = jnp.zeros(halo_sums.shape, F32)

    @pl.when(info[0] == groups - 1)
    def _():
        unpack_stored(place, j, cap, stored, planes, packed, sems, wide)
        each_slice(
            slices,
            lambda s: each_chunk(side, lambda a: collect(place, s, a, planes, h_last, own_sums, halo_sums)),
        )

    @pl.when(info[0] != groups - 1)
    def _():
        wave[...] = received[...]

        def one_slice(s):
            back(j, wave, col_mat, row_mat, rhs, h_buf, s)

            @pl.when(s > 0)
            def _():
                each_chunk(side, lambda a: leave(place, s, a, obj, halo, h_buf, wave))

            each_chunk(side, lambda a: collect(place, s, a, planes_in, h_buf, own_sums, halo_sums))

        each_slice(slices, one_slice)


def rims_kernel(info, own_sums, halo_sums, cross_rim, chip_rim, own):
    side = info[1] % 2
    cross_rim[...] = halo_sums[side].astype(BF16)
    chip_rim[...] = halo_sums[1 - side].astype(BF16)
    own[...] = own_sums[...].astype(BF16)


def add_rim(own, ct, rim, mix, s):
    _, _, parts, rows, _ = own.shape
    for c in range(parts):
        total = own[ct, s, c].astype(F32) + rim[s, c].astype(F32)
        mix[pl.ds(s * rows * 4 + ct * 2 + c, rows, stride=4), :] = total


def inside_kernel(info, own, rim, mix):
    for s in range(own.shape[1]):
        add_rim(own, 1 - info[1] % 2, rim, mix, s)


def close_kernel(info, own, rim, mix_in, out, mix, packed, sems):
    slices = own.shape[1]
    length = mix.shape[0] // slices
    copies = []
    for s in range(slices):
        part = pl.ds(s * length, length)
        add_rim(own, info[1] % 2, rim, mix, s)
        packed[part, :] = mix[part, :].astype(BF16)
        copies.append(pltpu.make_async_copy(packed.at[part], out.at[part], sems.at[s]))
        copies[-1].start()
    for copy in copies:
        copy.wait()


def near(x):
    return pltpu.with_memory_space_constraint(x, pltpu.VMEM)


def far(x):
    return pltpu.with_memory_space_constraint(x, pltpu.HBM)


def kernel_call(body, scalars, arrays, out, scratch=(), aliases=None, mib=8, distant=()):
    single = not isinstance(out, tuple)
    specs = tuple(SMEM if o.memory_space == pltpu.SMEM else VMEM for o in ((out,) if single else out))
    return pl.pallas_call(
        body,
        out_shape=out,
        in_specs=[SMEM] * len(scalars) + [HBM] * len(distant) + [VMEM] * len(arrays),
        out_specs=specs[0] if single else specs,
        scratch_shapes=list(scratch),
        input_output_aliases=aliases or {},
        compiler_params=pltpu.CompilerParams(vmem_limit_bytes=mib << 20),
    )(*scalars, *[far(a) for a in distant], *[near(a) for a in arrays])


def on_device(exit_grad, stored_waves, object_slices, propagator_taps, positions, counts):
    slices, cap, side = stored_waves.shape[:3]
    rows = object_slices.shape[1]
    groups = lax.axis_size("depth")
    tiles = lax.axis_size("tile")
    group_index = lax.axis_index("depth")
    across = [(i, (i + 1) % tiles if i % 2 else (i - 1) % tiles) for i in range(tiles)]
    inside = [(i, i ^ 1) for i in range(tiles)]

    def moved(x, pairs):
        return lax.ppermute(x, "tile", pairs)

    def swap(x, one, other):
        return lax.ppermute(x, "depth", [(one, other), (other, one)])

    moved_exits = [swap(exit_grad, g, groups - 1) for g in range(groups - 1)]
    exits = [as_rows(x) for x in moved_exits + [exit_grad]]

    obj_shape = pltpu.VMEM((slices * rows * 4, LANES), F32)
    wave_shape = pltpu.VMEM((side, 2 * side), BF16)
    wide_scratch = pltpu.VMEM((side * 4, LANES), F32)
    edge_shapes = (pltpu.VMEM((slices, 2, rows, LANES), BF16),) * 2
    spots = positions.T
    pieces = slices * 2 if rows % (2 * PACKED) == 0 else slices
    cross_edge, chip_edge, info, taps, obj = pl.pallas_call(
        first_kernel,
        out_shape=(
            *edge_shapes,
            pltpu.SMEM((3 + 2 * cap,), jnp.int32),
            pltpu.SMEM(propagator_taps.shape, F32),
            obj_shape,
        ),
        in_specs=[HBM] * 4,
        out_specs=(VMEM, VMEM, SMEM, SMEM, VMEM),
        scratch_shapes=[
            pltpu.SMEM(counts.shape, jnp.int32),
            pltpu.SMEM(spots.shape, jnp.int32),
            pltpu.SemaphoreType.DMA((3,)),
            pltpu.SemaphoreType.DMA((pieces,)),
        ],
        compiler_params=pltpu.CompilerParams(vmem_limit_bytes=8 << 20),
        name="first",
    )(*[far(a) for a in (counts, spots, propagator_taps, as_rows(object_slices))])
    from_across = moved(cross_edge, across)
    from_inside = moved(chip_edge, inside)

    col_mats, row_mat = kernel_call(
        matrices_kernel,
        (info, taps),
        (),
        (pltpu.VMEM((cap, 2 * side, 2 * side), BF16), wave_shape),
        (pltpu.VMEM((4, 3, LANES, LANES), F32),),
    )
    mats = (col_mats, row_mat)
    stored = as_rows(stored_waves)
    rhs_scratch = pltpu.VMEM((2 * side, 2 * side), BF16)
    h_shape = pltpu.VMEM((slices, side, 2 * side), F32)
    halo_shape = pltpu.VMEM((slices, 2, side + PACKED, LANES), F32)
    planes_shape = pltpu.VMEM((slices, 2, side, side), BF16)
    sums_shape = pltpu.VMEM((2, slices, 2, rows, LANES), F32)

    packed_scratch = (
        pltpu.VMEM((slices, side * 4, LANES), BF16),
        pltpu.SemaphoreType.DMA((slices,)),
    )
    h_start = kernel_call(
        functools.partial(start_kernel, groups, len(exits)),
        (info,),
        (*mats, *exits),
        pltpu.VMEM((1, side, 2 * side), F32),
        (wave_shape, wide_scratch, rhs_scratch),
    )

    def resume():
        return kernel_call(
            functools.partial(resume_kernel, groups),
            (info,),
            (obj, from_across, from_inside, *mats, h_start),
            (wave_shape, h_shape, planes_shape, halo_shape),
            (rhs_scratch, wide_scratch, *packed_scratch),
            distant=(stored,),
        )

    def forward(j, group, incoming):
        return kernel_call(
            functools.partial(forward_kernel, groups, j, group, len(incoming)),
            (info,),
            (obj, from_across, from_inside, *mats, *incoming),
            (wave_shape, h_shape, planes_shape, halo_shape),
            (wide_scratch, rhs_scratch, *packed_scratch),
            distant=(stored,),
        )

    def gradient(j, received, h_last, planes, halo, sums):
        return kernel_call(
            functools.partial(grad_kernel, groups, j),
            (info,),
            (obj, *mats, halo, planes, received, h_last, *sums),
            (sums_shape, sums_shape),
            (wave_shape, rhs_scratch, h_shape, planes_shape, wide_scratch, *packed_scratch),
            {9: 0, 10: 1} if sums else {},
            distant=(stored,),
        )

    def with_live(live):
        def run():
            ready = [resume()]
            waves = [None] * live
            received = [None] * live
            for group in range(groups - 1, 0, -1):
                for j in range(live):
                    last = group == groups - 1
                    if not last:
                        sent = forward(j, group, [waves[j]])[0]
                    else:
                        if j > 0:
                            ready.append(forward(j, group, exits))
                        sent = ready[j][0]
                    arrived = swap(sent, group, group - 1)
                    waves[j] = arrived
                    mine = group_index == group - 1
                    received[j] = arrived if last else jnp.where(mine, arrived, received[j])
            sums = ()
            for j in range(live):
                sums = gradient(j, received[j], *ready[j][1:], sums)
            own_shape = pltpu.VMEM((2, slices, 2, rows, LANES), BF16)
            return kernel_call(rims_kernel, (info,), sums, (*edge_shapes, own_shape))

        return run

    cross_rim, chip_rim, own = lax.switch(info[2] - 1, [with_live(n + 1) for n in range(cap)])
    rim_across = moved(cross_rim, across)
    rim_inside = moved(chip_rim, inside)
    mix_shape = pltpu.VMEM((slices * rows * 4, LANES), F32)
    mix = kernel_call(inside_kernel, (info,), (own, rim_inside), mix_shape)
    out_rows, _ = pl.pallas_call(
        close_kernel,
        out_shape=(jax.ShapeDtypeStruct((slices * rows * 4, LANES), BF16), mix_shape),
        in_specs=[SMEM, VMEM, VMEM, VMEM],
        out_specs=(HBM, VMEM),
        scratch_shapes=[
            pltpu.VMEM((slices * rows * 4, LANES), BF16),
            pltpu.SemaphoreType.DMA((slices,)),
        ],
        input_output_aliases={3: 1},
        compiler_params=pltpu.CompilerParams(vmem_limit_bytes=8 << 20),
        name="close",
    )(info, near(own), near(rim_across), near(mix))
    return from_rows(out_rows, (slices, rows, 2, 2 * LANES))


def solution(mesh):
    return jax.shard_map(
        on_device,
        mesh=mesh,
        in_specs=(
            P("tile", "depth", None, None),
            P("depth", "tile", None, None, None),
            P("depth", None, None, "tile"),
            P(),
            P(),
            P(),
        ),
        out_specs=P("depth", None, None, "tile"),
        check_vma=False,
    )
```

```python
import functools

import jax
import jax.numpy as jnp
from jax import lax
from jax.experimental import pallas as pl
from jax.experimental.pallas import tpu as pltpu
from jax.sharding import PartitionSpec as P


LANES = 128
CHUNK = 64
WIDE_CHUNK = 256
STEP = 32
PACKED = 16
F32 = jnp.float32
BF16 = jnp.bfloat16
VMEM = pl.BlockSpec(memory_space=pltpu.VMEM)
SMEM = pl.BlockSpec(memory_space=pltpu.SMEM)
HBM = pl.BlockSpec(memory_space=pltpu.HBM)


def as_rows(x):
    *lead, parts, columns = x.shape
    tiles = columns // LANES
    split = x.reshape(*lead, parts, tiles, LANES)
    return jnp.swapaxes(split, -3, -2).reshape(-1, LANES)


def from_rows(x, shape):
    *lead, parts, columns = shape
    tiles = columns // LANES
    split = x.reshape(*lead, tiles, parts, LANES)
    return jnp.swapaxes(split, -3, -2).reshape(shape)


def row_ids(start, rows):
    return lax.broadcasted_iota(jnp.int32, (rows, LANES), 0) + start


def lane_ids(rows):
    return lax.broadcasted_iota(jnp.int32, (rows, LANES), 1)


class Place:
    def __init__(self, info, j, cap):
        self.row = info[3 + j]
        self.col = info[3 + cap + j]
        self.mixed = jnp.where(self.col < LANES, 0, 1)

    def halo_first(self, total_rows, halo_rows):
        return pl.multiple_of(jnp.minimum(self.row // PACKED * PACKED, total_rows - halo_rows), PACKED)

    def on_halo(self, rows):
        column = lane_ids(rows) + self.mixed * LANES
        return (column >= self.col) == (self.mixed == 0)


def first_kernel(
    counts,
    positions,
    taps,
    obj_in,
    cross_edge,
    chip_edge,
    info,
    taps_out,
    obj,
    counts_in,
    spots,
    small_sem,
    obj_sem,
):
    cap = (info.shape[0] - 3) // 2
    slices, parts, rows, _ = cross_edge.shape
    pieces = obj_sem.shape[0]
    piece_rows = slices * rows // pieces

    def copy(source, target, sem):
        return pltpu.make_async_copy(source, target, sem)

    small = [
        copy(source, target, small_sem.at[i])
        for i, (source, target) in enumerate(((counts, counts_in), (positions, spots), (taps, taps_out)))
    ]
    loads = []
    for p in range(pieces):
        part = pl.ds(p * piece_rows * 4, piece_rows * 4)
        loads.append(copy(obj_in.at[part], obj.at[part], obj_sem.at[p]))
    for each in loads + small:
        each.start()
    tile = lax.axis_index("tile")
    cross_side = tile % 2
    for p in range(pieces):
        loads[p].wait()
        s, first = divmod(p * piece_rows, rows)
        start = p * piece_rows * 4
        for c in range(parts):
            beyond = obj[pl.ds(start + cross_side * 2 + c, piece_rows, stride=4), :]
            beside = obj[pl.ds(start + (1 - cross_side) * 2 + c, piece_rows, stride=4), :]
            cross_edge[s, c, pl.ds(first, piece_rows), :] = beyond.astype(BF16)
            chip_edge[s, c, pl.ds(first, piece_rows), :] = beside.astype(BF16)
    for each in small:
        each.wait()
    info[0] = lax.axis_index("depth")
    info[1] = tile
    info[2] = counts_in[tile]
    for j in range(cap):
        info[3 + j] = spots[0, tile * cap + j]
        info[3 + cap + j] = spots[1, tile * cap + j]


def build_blocks(taps, blocks):
    tap_count = taps.shape[2]
    centre = tap_count // 2

    def tap(m, k):
        return taps[1, m, k] if m < 2 else taps[0, m - 2, tap_count - 1 - k]

    def build(block, first, shift, ks):
        diff = lane_ids(STEP) - row_ids(first, STEP) + shift
        total = [jnp.zeros((STEP, LANES), F32) for _ in range(4)]
        for k in ks:
            hit = diff == k - centre
            for m in range(4):
                total[m] = jnp.where(hit, tap(m, k), total[m])
        for m in range(4):
            blocks[m, block, pl.ds(first, STEP), :] = total[m]

    def diagonal(i, carry):
        build(0, pl.multiple_of(i * STEP, STEP), 0, range(tap_count))
        return carry

    lax.fori_loop(0, LANES // STEP, diagonal, 0)
    for first in range(0, LANES, STEP):
        build(1, first, LANES, range(centre + 1, tap_count) if first + STEP == LANES else ())
        build(2, first, -LANES, range(centre) if first == 0 else ())


def matrices_kernel(info, taps, col_mat, row_mat, blocks):
    cap = col_mat.shape[0]
    side = row_mat.shape[0]
    build_blocks(taps, blocks)

    def rows_of(i, tile_row):
        return pl.ds(pl.multiple_of(i * STEP + tile_row * LANES, STEP), STEP)

    def low_rows_of(i, tile_row):
        return pl.ds(pl.multiple_of(i * STEP + tile_row * LANES + side, STEP), STEP)

    def row_part(i, carry):
        for tr in range(2):
            for tc in range(2):
                block = 0 if tr == tc else 1 + tr
                for c in range(2):
                    value = blocks[2 + c, block, pl.ds(pl.multiple_of(i * STEP, STEP), STEP), :]
                    row_mat[rows_of(i, tr), pl.ds(tc * LANES + c * side, LANES)] = value.astype(BF16)
        return carry

    lax.fori_loop(0, LANES // STEP, row_part, 0)

    def slot(j, carry):
        seam = Place(info, j, cap).col

        def fill(i, inner):
            first = pl.multiple_of(i * STEP, STEP)
            for tr in range(2):
                for tc in range(2):
                    row_side = row_ids(first, STEP) + tr * LANES >= seam
                    col_side = lane_ids(STEP) + tc * LANES >= seam
                    same = row_side == col_side
                    values = []
                    for m in range(2):
                        if tr == tc:
                            close, far = blocks[m, 0, pl.ds(first, STEP), :], 0.0
                        else:
                            close = blocks[m, 1 + tr, pl.ds(first, STEP), :]
                            far = blocks[m, 2 - tr, pl.ds(first, STEP), :]
                        values.append(jnp.where(same, close, far))
                    re, im = values[0].astype(BF16), values[1].astype(BF16)
                    re_cols = pl.ds(tc * LANES, LANES)
                    im_cols = pl.ds(tc * LANES + side, LANES)
                    col_mat[j, rows_of(i, tr), re_cols] = re
                    col_mat[j, rows_of(i, tr), im_cols] = -im
                    col_mat[j, low_rows_of(i, tr), re_cols] = im
                    col_mat[j, low_rows_of(i, tr), im_cols] = re
            return inner

        return lax.fori_loop(0, LANES // STEP, fill, carry)

    lax.fori_loop(0, info[2], slot, 0)


def take_halo(info, place, across, inside, halo):
    rows = pl.ds(place.halo_first(across.shape[2], halo.shape[2]), halo.shape[2])
    from_across = place.mixed == info[1] % 2

    @pl.when(from_across)
    def _():
        halo[...] = across[:, :, rows, :].astype(F32)

    @pl.when(jnp.logical_not(from_across))
    def _():
        halo[...] = inside[:, :, rows, :].astype(F32)


def unpack(place, sources, wide, write):
    side = 0
    for packed, start, count in sources:
        wide[pl.ds(side * 4, count * 4), :] = packed[pl.ds(start, count * 4), :].astype(F32)
        side += count

    def move(i, carry):
        a = pl.multiple_of(i * WIDE_CHUNK, WIDE_CHUNK)
        for c in range(2):
            halves = [wide[pl.ds(a * 4 + ct * 2 + c, WIDE_CHUNK, stride=4), :] for ct in range(2)]
            value = pltpu.roll(jnp.concatenate(halves, axis=1), place.col, 1)
            write(c, pl.ds(a, WIDE_CHUNK), value.astype(BF16))
        return carry

    lax.fori_loop(0, side // WIDE_CHUNK, move, 0)


def unpack_stored(place, j, cap, stored, planes, packed, sems, wide):
    slices, _, side, _ = planes.shape

    def load(s):
        start = pl.multiple_of((s * cap + j) * side * 4, side * 4)
        return pltpu.make_async_copy(stored.at[pl.ds(start, side * 4)], packed.at[s], sems.at[s])

    def begin(s, carry):
        load(s).start()
        return carry

    def one(s, carry):
        def write(c, rows, value):
            planes[s, c, rows] = value

        load(s).wait()
        unpack(place, [(packed.at[s], 0, side)], wide, write)
        return carry

    lax.fori_loop(0, slices, begin, 0)
    lax.fori_loop(0, slices, one, 0)


def back(j, wave, col_mat, row_mat, rhs, h_buf, s):
    side = wave.shape[0]
    mixed = jnp.dot(wave[...], col_mat[j], preferred_element_type=F32).astype(BF16)
    rhs[:side, :] = mixed
    rhs[side:, :side] = mixed[:, side:]
    rhs[side:, side:] = -mixed[:, :side]
    h_buf[s] = jnp.dot(row_mat[...], rhs[...], preferred_element_type=F32)


def tile_columns(ct, c, side):
    return pl.ds(pl.multiple_of(ct * LANES + c * side, LANES), LANES)


def leave(place, s, a, obj, halo, h_buf, wave):
    side = wave.shape[0]
    total_rows = obj.shape[0] // h_buf.shape[0] // 4
    halo_row = place.row - place.halo_first(total_rows, halo.shape[2]) + a
    rows = pl.ds(a, CHUNK)
    on_halo = place.on_halo(CHUNK)
    for ct, own in ((place.mixed, 1 - place.mixed), (1 - place.mixed, place.mixed)):
        o = []
        for c in range(2):
            first = (s * total_rows + place.row + a) * 4 + own * 2 + c
            value = obj[pl.ds(first, CHUNK, stride=4), :]
            if ct is place.mixed:
                beyond = halo[s, c, pl.ds(halo_row, CHUNK), :]
                value = jnp.where(on_halo, beyond, value)
            o.append(value)
        h_re = h_buf[s, rows, tile_columns(ct, 0, side)]
        h_im = h_buf[s, rows, tile_columns(ct, 1, side)]
        wave[rows, tile_columns(ct, 0, side)] = (o[0] * h_re + o[1] * h_im).astype(BF16)
        wave[rows, tile_columns(ct, 1, side)] = (o[0] * h_im - o[1] * h_re).astype(BF16)


def collect(place, s, a, planes, h_buf, own_sums, halo_sums):
    side = h_buf.shape[1]
    rows = pl.ds(a, CHUNK)
    frame_rows = pl.ds(place.row + a, CHUNK)
    on_halo = place.on_halo(CHUNK)
    for ct, own in ((place.mixed, 1 - place.mixed), (1 - place.mixed, place.mixed)):
        cols = tile_columns(ct, 0, side)
        st_re = planes[s, 0, rows, cols].astype(F32)
        st_im = planes[s, 1, rows, cols].astype(F32)
        h_re = h_buf[s, rows, cols]
        h_im = h_buf[s, rows, tile_columns(ct, 1, side)]
        for c, g in enumerate((st_re * h_re + st_im * h_im, st_re * h_im - st_im * h_re)):
            if ct is place.mixed:
                halo_sums[place.mixed, s, c, frame_rows, :] += jnp.where(on_halo, g, 0.0)
                own_sums[own, s, c, frame_rows, :] += jnp.where(on_halo, 0.0, g)
            else:
                own_sums[own, s, c, frame_rows, :] += g


def each_chunk(side, body):
    def step(k, carry):
        body(pl.multiple_of(k * CHUNK, CHUNK))
        return carry

    lax.fori_loop(0, side // CHUNK, step, 0)


def each_slice(slices, body):
    def step(i, carry):
        body(slices - 1 - i)
        return carry

    lax.fori_loop(0, slices, step, 0)


def take_exit(place, j, incoming, out, wide):
    side = out.shape[0]
    count = side // len(incoming)

    def write(c, rows, value):
        out[rows, pl.ds(c * side, side)] = value

    unpack(place, [(ref, j * count * 4, count) for ref in incoming], wide, write)


def start_kernel(groups, n_in, *refs):
    info, col_mat, row_mat = refs[:3]
    incoming = refs[3 : 3 + n_in]
    h_buf, out, wide, rhs = refs[3 + n_in :]
    place = Place(info, 0, col_mat.shape[0])

    @pl.when(info[0] == groups - 1)
    def _():
        take_exit(place, 0, incoming, out, wide)
        back(0, out, col_mat, row_mat, rhs, h_buf, 0)


def resume_kernel(
    groups,
    info,
    stored,
    obj,
    across,
    inside,
    col_mat,
    row_mat,
    old_h,
    out,
    h_buf,
    planes,
    halo,
    rhs,
    wide,
    packed,
    sems,
):
    slices, side = h_buf.shape[:2]
    place = Place(info, 0, col_mat.shape[0])
    take_halo(info, place, across, inside, halo)

    @pl.when(info[0] == groups - 1)
    def _():
        h_buf[slices - 1] = old_h[0]

        def one_slice(s):
            each_chunk(side, lambda a: leave(place, s, a, obj, halo, h_buf, out))

            @pl.when(s > 0)
            def _():
                back(0, out, col_mat, row_mat, rhs, h_buf, s - 1)

        each_slice(slices, one_slice)

    @pl.when(info[0] != groups - 1)
    def _():
        unpack_stored(place, 0, col_mat.shape[0], stored, planes, packed, sems, wide)


def forward_kernel(groups, j, group, n_in, *refs):
    info, stored, obj, across, inside, col_mat, row_mat = refs[:7]
    incoming = refs[7 : 7 + n_in]
    out, h_buf, planes, halo, wide, rhs, packed, sems = refs[7 + n_in :]
    slices, side = h_buf.shape[:2]
    cap = col_mat.shape[0]
    last = group == groups - 1
    place = Place(info, j, cap)
    take_halo(info, place, across, inside, halo)

    @pl.when(info[0] == group)
    def _():
        if last:
            take_exit(place, j, incoming, out, wide)
        else:
            out[...] = incoming[0][...]

        def one_slice(s):
            back(j, out, col_mat, row_mat, rhs, h_buf, s)
            each_chunk(side, lambda a: leave(place, s, a, obj, halo, h_buf, out))

        each_slice(slices, one_slice)

    if last:

        @pl.when(info[0] != group)
        def _():
            unpack_stored(place, j, cap, stored, planes, packed, sems, wide)


def grad_kernel(groups, j, *refs):
    info, stored, obj, col_mat, row_mat, halo, planes_in, received, h_last = refs[:9]
    own_sums, halo_sums, wave, rhs, h_buf, planes, wide, packed, sems = refs[-9:]
    slices, side = h_last.shape[:2]
    cap = col_mat.shape[0]
    place = Place(info, j, cap)
    if j == 0:
        own_sums[...] = jnp.zeros(own_sums.shape, F32)
        halo_sums[...] = jnp.zeros(halo_sums.shape, F32)

    @pl.when(info[0] == groups - 1)
    def _():
        unpack_stored(place, j, cap, stored, planes, packed, sems, wide)
        each_slice(
            slices,
            lambda s: each_chunk(side, lambda a: collect(place, s, a, planes, h_last, own_sums, halo_sums)),
        )

    @pl.when(info[0] != groups - 1)
    def _():
        wave[...] = received[...]

        def one_slice(s):
            back(j, wave, col_mat, row_mat, rhs, h_buf, s)

            @pl.when(s > 0)
            def _():
                each_chunk(side, lambda a: leave(place, s, a, obj, halo, h_buf, wave))

            each_chunk(side, lambda a: collect(place, s, a, planes_in, h_buf, own_sums, halo_sums))

        each_slice(slices, one_slice)


def rims_kernel(info, own_sums, halo_sums, cross_rim, chip_rim, own):
    side = info[1] % 2
    cross_rim[...] = halo_sums[side].astype(BF16)
    chip_rim[...] = halo_sums[1 - side].astype(BF16)
    own[...] = own_sums[...].astype(BF16)


def add_rim(own, ct, rim, mix, s):
    _, _, parts, rows, _ = own.shape
    for c in range(parts):
        total = own[ct, s, c].astype(F32) + rim[s, c].astype(F32)
        mix[pl.ds(s * rows * 4 + ct * 2 + c, rows, stride=4), :] = total


def inside_kernel(info, own, rim, mix):
    for s in range(own.shape[1]):
        add_rim(own, 1 - info[1] % 2, rim, mix, s)


def close_kernel(info, own, rim, mix_in, out, mix, packed, sems):
    slices = own.shape[1]
    length = mix.shape[0] // slices
    copies = []
    for s in range(slices):
        part = pl.ds(s * length, length)
        add_rim(own, info[1] % 2, rim, mix, s)
        packed[part, :] = mix[part, :].astype(BF16)
        copies.append(pltpu.make_async_copy(packed.at[part], out.at[part], sems.at[s]))
        copies[-1].start()
    for copy in copies:
        copy.wait()


def near(x):
    return pltpu.with_memory_space_constraint(x, pltpu.VMEM)


def far(x):
    return pltpu.with_memory_space_constraint(x, pltpu.HBM)


def kernel_call(body, scalars, arrays, out, scratch=(), aliases=None, mib=8, distant=()):
    single = not isinstance(out, tuple)
    specs = tuple(SMEM if o.memory_space == pltpu.SMEM else VMEM for o in ((out,) if single else out))
    return pl.pallas_call(
        body,
        out_shape=out,
        in_specs=[SMEM] * len(scalars) + [HBM] * len(distant) + [VMEM] * len(arrays),
        out_specs=specs[0] if single else specs,
        scratch_shapes=list(scratch),
        input_output_aliases=aliases or {},
        compiler_params=pltpu.CompilerParams(vmem_limit_bytes=mib << 20),
    )(*scalars, *[far(a) for a in distant], *[near(a) for a in arrays])


def on_device(exit_grad, stored_waves, object_slices, propagator_taps, positions, counts):
    slices, cap, side = stored_waves.shape[:3]
    rows = object_slices.shape[1]
    groups = lax.axis_size("depth")
    tiles = lax.axis_size("tile")
    group_index = lax.axis_index("depth")
    across = [(i, (i + 1) % tiles if i % 2 else (i - 1) % tiles) for i in range(tiles)]
    inside = [(i, i ^ 1) for i in range(tiles)]

    def moved(x, pairs):
        return lax.ppermute(x, "tile", pairs)

    def swap(x, one, other):
        return lax.ppermute(x, "depth", [(one, other), (other, one)])

    moved_exits = [swap(exit_grad, g, groups - 1) for g in range(groups - 1)]
    exits = [as_rows(x) for x in moved_exits + [exit_grad]]

    obj_shape = pltpu.VMEM((slices * rows * 4, LANES), F32)
    wave_shape = pltpu.VMEM((side, 2 * side), BF16)
    wide_scratch = pltpu.VMEM((side * 4, LANES), F32)
    edge_shapes = (pltpu.VMEM((slices, 2, rows, LANES), BF16),) * 2
    spots = positions.T
    pieces = slices * 2 if rows % (2 * PACKED) == 0 else slices
    cross_edge, chip_edge, info, taps, obj = pl.pallas_call(
        first_kernel,
        out_shape=(
            *edge_shapes,
            pltpu.SMEM((3 + 2 * cap,), jnp.int32),
            pltpu.SMEM(propagator_taps.shape, F32),
            obj_shape,
        ),
        in_specs=[HBM] * 4,
        out_specs=(VMEM, VMEM, SMEM, SMEM, VMEM),
        scratch_shapes=[
            pltpu.SMEM(counts.shape, jnp.int32),
            pltpu.SMEM(spots.shape, jnp.int32),
            pltpu.SemaphoreType.DMA((3,)),
            pltpu.SemaphoreType.DMA((pieces,)),
        ],
        compiler_params=pltpu.CompilerParams(vmem_limit_bytes=8 << 20),
        name="first",
    )(*[far(a) for a in (counts, spots, propagator_taps, as_rows(object_slices))])
    from_across = moved(cross_edge, across)
    from_inside = moved(chip_edge, inside)

    col_mats, row_mat = kernel_call(
        matrices_kernel,
        (info, taps),
        (),
        (pltpu.VMEM((cap, 2 * side, 2 * side), BF16), wave_shape),
        (pltpu.VMEM((4, 3, LANES, LANES), F32),),
    )
    mats = (col_mats, row_mat)
    stored = as_rows(stored_waves)
    rhs_scratch = pltpu.VMEM((2 * side, 2 * side), BF16)
    h_shape = pltpu.VMEM((slices, side, 2 * side), F32)
    halo_shape = pltpu.VMEM((slices, 2, side + PACKED, LANES), F32)
    planes_shape = pltpu.VMEM((slices, 2, side, side), BF16)
    sums_shape = pltpu.VMEM((2, slices, 2, rows, LANES), F32)

    packed_scratch = (
        pltpu.VMEM((slices, side * 4, LANES), BF16),
        pltpu.SemaphoreType.DMA((slices,)),
    )
    h_start = kernel_call(
        functools.partial(start_kernel, groups, len(exits)),
        (info,),
        (*mats, *exits),
        pltpu.VMEM((1, side, 2 * side), F32),
        (wave_shape, wide_scratch, rhs_scratch),
    )

    def resume():
        return kernel_call(
            functools.partial(resume_kernel, groups),
            (info,),
            (obj, from_across, from_inside, *mats, h_start),
            (wave_shape, h_shape, planes_shape, halo_shape),
            (rhs_scratch, wide_scratch, *packed_scratch),
            distant=(stored,),
        )

    def forward(j, group, incoming):
        return kernel_call(
            functools.partial(forward_kernel, groups, j, group, len(incoming)),
            (info,),
            (obj, from_across, from_inside, *mats, *incoming),
            (wave_shape, h_shape, planes_shape, halo_shape),
            (wide_scratch, rhs_scratch, *packed_scratch),
            distant=(stored,),
        )

    def gradient(j, received, h_last, planes, halo, sums):
        return kernel_call(
            functools.partial(grad_kernel, groups, j),
            (info,),
            (obj, *mats, halo, planes, received, h_last, *sums),
            (sums_shape, sums_shape),
            (wave_shape, rhs_scratch, h_shape, planes_shape, wide_scratch, *packed_scratch),
            {9: 0, 10: 1} if sums else {},
            distant=(stored,),
        )

    def with_live(live):
        def run():
            ready = [resume()]
            waves = [None] * live
            received = [None] * live
            for group in range(groups - 1, 0, -1):
                for j in range(live):
                    last = group == groups - 1
                    if not last:
                        sent = forward(j, group, [waves[j]])[0]
                    else:
                        if j > 0:
                            ready.append(forward(j, group, exits))
                        sent = ready[j][0]
                    arrived = swap(sent, group, group - 1)
                    waves[j] = arrived
                    mine = group_index == group - 1
                    received[j] = arrived if last else jnp.where(mine, arrived, received[j])
            sums = ()
            for j in range(live):
                sums = gradient(j, received[j], *ready[j][1:], sums)
            own_shape = pltpu.VMEM((2, slices, 2, rows, LANES), BF16)
            return kernel_call(rims_kernel, (info,), sums, (*edge_shapes, own_shape))

        return run

    cross_rim, chip_rim, own = lax.switch(info[2] - 1, [with_live(n + 1) for n in range(cap)])
    rim_across = moved(cross_rim, across)
    rim_inside = moved(chip_rim, inside)
    mix_shape = pltpu.VMEM((slices * rows * 4, LANES), F32)
    mix = kernel_call(inside_kernel, (info,), (own, rim_inside), mix_shape)
    out_rows, _ = pl.pallas_call(
        close_kernel,
        out_shape=(jax.ShapeDtypeStruct((slices * rows * 4, LANES), BF16), mix_shape),
        in_specs=[SMEM, VMEM, VMEM, VMEM],
        out_specs=(HBM, VMEM),
        scratch_shapes=[
            pltpu.VMEM((slices * rows * 4, LANES), BF16),
            pltpu.SemaphoreType.DMA((slices,)),
        ],
        input_output_aliases={3: 1},
        compiler_params=pltpu.CompilerParams(vmem_limit_bytes=8 << 20),
        name="close",
    )(info, near(own), near(rim_across), near(mix))
    return from_rows(out_rows, (slices, rows, 2, 2 * LANES))


def solution(mesh):
    return jax.shard_map(
        on_device,
        mesh=mesh,
        in_specs=(
            P("tile", "depth", None, None),
            P("depth", "tile", None, None, None),
            P("depth", None, None, "tile"),
            P(),
            P(),
            P(),
        ),
        out_specs=P("depth", None, None, "tile"),
        check_vma=False,
    )
```
